32 devices in a mesh: heads: 4 (over y, x), rows: 8 (over z, core).
Axes of the slice: x: 2, y: 2, z: 4, core: 2. Of those that a mesh axis runs over, the one named last changes fastest.
Arguments:
- hidden_in: bfloat16 [8, 1024, 2048], P('rows', 'heads'), may hold values from -6 to 6
- segment_ids: int32 [8, 1024], P('rows'), may hold values from 0 to 7, never falling along the last dimension, each value on 1 to 256 neighbouring positions
- attn_gain: float32 [2048], replicated, may hold values from 0.5 to 1.5
- w_query: bfloat16 [2048, 1280], P(('heads', 'rows')), may hold values from -0.125 to 0.125
- w_key: bfloat16 [2048, 320], P(('heads', 'rows')), may hold values from -0.125 to 0.125
- w_value: bfloat16 [2048, 320], P(('heads', 'rows')), may hold values from -0.125 to 0.125
- query_gain: float32 [64], replicated, may hold values from 0.1 to 1.9
- key_gain: float32 [64], replicated, may hold values from 0.1 to 1.9
- w_out: bfloat16 [2048, 1280], P(('heads', 'rows')), may hold values from -0.625 to 0.625
- ffn_gain: float32 [2048], replicated, may hold values from 0.5 to 1.5
- w_gate: bfloat16 [2048, 3584], P(('heads', 'rows')), may hold values from -0.125 to 0.125
- w_up: bfloat16 [2048, 3584], P(('heads', 'rows')), may hold values from -0.125 to 0.125
- w_down: bfloat16 [2048, 3584], P(('heads', 'rows')), may hold values from -0.09375 to 0.09375
- cotangent: bfloat16 [8, 1024, 2048], P('rows', 'heads'), may hold values from -6 to 6
Outputs:
- layer_out: bfloat16 [8, 1024, 2048], P('rows', 'heads')
- grad_in: bfloat16 [8, 1024, 2048], P('rows', 'heads')
- grad_attn_gain: float32 [2048], P(('heads', 'rows'))
- grad_query: float32 [2048, 1280], P(('heads', 'rows'))
- grad_key: float32 [2048, 320], P(('heads', 'rows'))
- grad_value: float32 [2048, 320], P(('heads', 'rows'))
- grad_query_gain: float32 [64], replicated
- grad_key_gain: float32 [64], replicated
- grad_out: float32 [2048, 1280], P(('heads', 'rows'))
- grad_ffn_gain: float32 [2048], P(('heads', 'rows'))
- grad_gate: float32 [2048, 3584], P(('heads', 'rows'))
- grad_up: float32 [2048, 3584], P(('heads', 'rows'))
- grad_down: float32 [2048, 3584], P(('heads', 'rows'))
The draws below stay inside these ranges and needn't reach their ends.
Inputs may be any that keep to these rules, and one draw needn't show every extreme that they name: `segment_ids`: document numbers never fall along a sequence; a document has 1 to 256 tokens.
All inputs are finite; a program needn't handle non-finite values.
Results may differ from the reference program's by a relative error of at most 0.022.
Values may be sent and summed in bfloat16 or wider, within the bound.
No kernel may reach another device: no remote copies, remote signals or barrier semaphores. Data moves between devices by JAX's collectives and lax.ppermute only.
A program may use at most 320 MiB of HBM per device.

```python
import math
import jax
import jax.numpy as jnp
import numpy as np
from jax import lax

D = 2048
FF = 3584
QH = 20
KVH = 5
HD = 64
SEQ = 1024
SEQS = 8


def block_scale(key, dims, cuts, least, top_value):
    def one(dim, shards_of):
        draws = jax.random.uniform(jax.random.fold_in(jax.random.fold_in(key, 6), dim), (shards_of,), jnp.float32, least / len(cuts), top_value / len(cuts))
        return jnp.repeat(jnp.exp(draws), dims[dim] // shards_of).reshape((-1,) + (1,) * (len(dims) - dim - 1))

    loudness = one(*cuts[0])
    for cut in cuts[1:]:
        loudness = loudness * one(*cut)
    return loudness


def split_up(count, total, reach, skew):
    portions = [(1 << 20) // math.isqrt(standing ** skew) + 1 for standing in range(2, count + 1)]
    surplus, holding = total - reach - (count - 1), [1] * (count - 1)
    while surplus > 0:
        movable = [i for i in range(count - 1) if holding[i] < reach]
        whole, budget = sum([portions[i] for i in movable]), surplus
        for i in movable:
            extra = min(reach - holding[i], max(1, budget * portions[i] // whole), surplus)
            holding[i] = holding[i] + extra
            surplus = surplus - extra
    return np.array([reach] + holding)


def uneven(stream_key, count, total, bound, skew):
    if count == 2:
        one = jax.random.randint(stream_key, (), max(1, total - bound), min(bound, total - 1) + 1)
        return jnp.stack([one, total - one])
    tallies = jnp.asarray(split_up(count, total, bound, skew), jnp.int32)
    twos = (count - 1) // 2
    giver, taker = tallies[1:1 + 2 * twos:2], tallies[2:2 + 2 * twos:2]
    slack = jnp.minimum(giver - 1, bound - taker)
    moved = jax.random.randint(jax.random.fold_in(stream_key, 1), (twos,), 0, 1 << 20) % (slack + 1)
    tallies = tallies.at[1:1 + 2 * twos:2].set(giver - moved).at[2:2 + 2 * twos:2].set(taker + moved)
    return tallies[jax.random.permutation(jax.random.fold_in(stream_key, 2), count)]


def noise(key, dims, width, bound, cuts=(), kind=jnp.bfloat16):
    entries = width * jax.random.normal(key, dims, jnp.float32)
    if cuts:
        entries = entries * block_scale(key, dims, cuts, -0.22, 0.18)
    return jnp.clip(entries, -bound, bound).astype(kind)


def setup_inputs(seed: int = 0) -> dict:
    key_of = jax.random.split(jax.random.key(seed), 15)
    hidden_in = noise(key_of[0], (SEQS, SEQ, D), 1.0, 6.0, ((0, 8), (1, 4)))
    segment_ids = jax.vmap(lambda own: jnp.searchsorted(jnp.cumsum(uneven(own, 8, SEQ, SEQ // 4, 0)), jnp.arange(SEQ), side="right"))(jax.random.split(key_of[1], SEQS)).reshape((SEQS, SEQ)).astype(jnp.int32)
    attn_gain = jnp.clip(1.0 + 0.1 * jax.random.normal(key_of[2], (D,), jnp.float32), 0.5, 1.5)
    w_query = noise(key_of[3], (D, QH * HD), D ** -0.5, 0.125, ((0, 32),))
    w_key = noise(key_of[4], (D, KVH * HD), D ** -0.5, 0.125, ((0, 32),))
    w_value = noise(key_of[5], (D, KVH * HD), D ** -0.5, 0.125, ((0, 32),))
    query_gain = jnp.clip(1.0 + 0.18 * jax.random.normal(key_of[6], (HD,), jnp.float32), 0.1, 1.9)
    key_gain = jnp.clip(1.0 + 0.18 * jax.random.normal(key_of[7], (HD,), jnp.float32), 0.1, 1.9)
    w_out = noise(key_of[8], (D, QH * HD), (QH * HD // 16) ** -0.5, 0.625, ((0, 32),))
    ffn_gain = jnp.clip(1.0 + 0.1 * jax.random.normal(key_of[9], (D,), jnp.float32), 0.5, 1.5)
    w_gate = noise(key_of[10], (D, FF), D ** -0.5, 0.125, ((0, 32),))
    w_up = noise(key_of[11], (D, FF), D ** -0.5, 0.125, ((0, 32),))
    w_down = noise(key_of[12], (D, FF), FF ** -0.5, 0.09375, ((0, 32),))
    cotangent = noise(key_of[13], (SEQS, SEQ, D), 1.0, 6.0, ((0, 8), (1, 4)))
    return dict(hidden_in=hidden_in, segment_ids=segment_ids, attn_gain=attn_gain, w_query=w_query, w_key=w_key, w_value=w_value, query_gain=query_gain, key_gain=key_gain, w_out=w_out, ffn_gain=ffn_gain, w_gate=w_gate, w_up=w_up, w_down=w_down, cotangent=cotangent)


EPS = 1e-06
NEG = -1e+30
THETA = 10000.0
HIGH = lax.Precision.HIGHEST

@jax.custom_vjp
def low(v):
    return lax.optimization_barrier(v.astype(jnp.bfloat16)).astype(jnp.float32)

@jax.custom_vjp
def low_back(v):
    return v

def low_keep(v):
    return (low(v), None)

def low_pass(kept, grad):
    return (grad,)

def back_keep(v):
    return (v, None)

def back_low(kept, grad):
    return (low(grad),)
low.defvjp(low_keep, low_pass)
low_back.defvjp(back_keep, back_low)

def product(left, right):
    return jnp.dot(left, right, precision=HIGH, preferred_element_type=jnp.float32)

def unit_rows(v):
    return v * lax.rsqrt(lax.optimization_barrier(jnp.mean(v * v, axis=-1, keepdims=True)) + EPS)

def doc_positions(segs):
    places = jnp.arange(segs.shape[0], dtype=jnp.int32)
    first = jnp.concatenate([jnp.ones((1,), jnp.int32), (segs[1:] != segs[:-1]).astype(jnp.int32)])
    return places - lax.cummax(places * first, axis=0)

def rotary(positions):
    half = HD // 2
    freqs = jnp.exp(jnp.arange(half, dtype=jnp.float32) * (-2.0 * math.log(THETA) / HD))
    angles = positions.astype(jnp.float32)[:, None] * freqs[None, :]
    angles = jnp.concatenate([angles, angles], axis=-1)
    return (jnp.cos(angles), jnp.sin(angles))

def turn(v, cosine, sine):
    half = HD // 2
    turned = jnp.concatenate([-v[..., half:], v[..., :half]], axis=-1)
    return v * cosine[:, None, :] + turned * sine[:, None, :]

def forward(x, segs, g_one, w_q, w_k, w_v, g_q, g_k, w_o, g_two, w_g, w_u, w_d):
    length = x.shape[0]
    normed = low(unit_rows(x) * g_one)
    queries = low_back(product(normed, w_q)).reshape(length, QH, HD)
    keys = low_back(product(normed, w_k)).reshape(length, KVH, HD)
    values = low(low_back(product(normed, w_v))).reshape(length, KVH, HD)
    cosine, sine = rotary(doc_positions(segs))
    q_rot = low(turn(unit_rows(queries) * g_q, cosine, sine))
    k_rot = low(turn(unit_rows(keys) * g_k, cosine, sine))
    k_rep = jnp.repeat(k_rot, QH // KVH, axis=1)
    v_rep = jnp.repeat(values, QH // KVH, axis=1)
    scores = jnp.einsum('qhd,khd->hqk', q_rot, k_rep, precision=HIGH) * HD ** (-0.5)
    places = jnp.arange(length)
    allowed = (segs[:, None] == segs[None, :]) & (places[:, None] >= places[None, :])
    scores = low_back(jnp.where(allowed[None], scores, NEG))
    top = lax.optimization_barrier(jnp.max(scores, axis=-1, keepdims=True))
    expd = jnp.exp(scores - top)
    probs = low(expd / lax.optimization_barrier(jnp.sum(expd, axis=-1, keepdims=True)))
    mixed = jnp.einsum('hqk,khd->qhd', probs, v_rep, precision=HIGH)
    mixed = low(low_back(mixed)).reshape(length, QH * HD)
    attn = low_back(product(mixed, w_o.T))
    resid = x + attn
    normed_two = low(unit_rows(resid) * g_two)
    gate = low_back(product(normed_two, w_g))
    up = low_back(product(normed_two, w_u))
    hidden = low(gate * jax.nn.sigmoid(gate) * up)
    return resid + product(hidden, w_d.T)

def reference(hidden_in, segment_ids, attn_gain, w_query, w_key, w_value, query_gain, key_gain, w_out, ffn_gain, w_gate, w_up, w_down, cotangent):
    params = tuple((p.astype(jnp.float32) for p in (attn_gain, w_query, w_key, w_value, query_gain, key_gain, w_out, ffn_gain, w_gate, w_up, w_down)))

    def one_sequence(carry, items):
        x_seq, segs, grad_seq = items

        def run(x, *weights):
            return forward(x, segs, *weights)
        result, pull = jax.vjp(run, x_seq.astype(jnp.float32), *params)
        grads = pull(grad_seq.astype(jnp.float32))
        summed = tuple((c + g for c, g in zip(carry, grads[1:])))
        return (summed, (result.astype(jnp.bfloat16), grads[0].astype(jnp.bfloat16)))
    start = tuple((jnp.zeros_like(p) for p in params))
    sums, outputs = lax.scan(one_sequence, start, (hidden_in, segment_ids, cotangent))
    layer_out, grad_in = outputs
    return (layer_out, grad_in, sums[0], sums[1], sums[2], sums[3], sums[4], sums[5], sums[6], sums[7], sums[8], sums[9], sums[10])
```

```python
import math

import jax
import jax.numpy as jnp
from jax import lax
from jax.sharding import Mesh
from jax.sharding import PartitionSpec as P

HD = 64
EPS = 1e-06
NEG = -1e30
THETA = 10000.0
ROWS = ("zz", "core")
ALL = ("heads", "zz", "core")
F32 = jnp.float32
BF16 = jnp.bfloat16


def norm_scale(v):
    return lax.rsqrt(jnp.mean(v * v, axis=-1, keepdims=True) + EPS)


def norm_back(grad_n, unit_v, scale, gain):
    scaled = grad_n * gain
    return scale * (scaled - unit_v * jnp.mean(scaled * unit_v, axis=-1, keepdims=True))


def positions_of(segment_ids):
    places = lax.broadcasted_iota(jnp.int32, segment_ids.shape, 0)
    first = jnp.concatenate(
        [jnp.ones_like(segment_ids[:1]), (segment_ids[1:] != segment_ids[:-1]).astype(jnp.int32)]
    )
    return places - lax.cummax(places * first, axis=0)


def rotary_tables(positions):
    half = HD // 2
    freqs = jnp.exp(jnp.arange(half, dtype=F32) * (-2.0 * math.log(THETA) / HD))
    angles = positions.astype(F32)[:, None] * freqs
    angles = jnp.concatenate([angles, angles], axis=-1)
    return jnp.cos(angles), jnp.sin(angles)


def rotate(v, cosine, sine):
    half = HD // 2
    turned = jnp.concatenate([-v[..., half:], v[..., :half]], axis=-1)
    return v * cosine[:, None, :] + turned * sine[:, None, :]


def rotate_back(grad, cosine, sine):
    half = HD // 2
    scaled = grad * sine[:, None, :]
    back = jnp.concatenate([scaled[..., half:], -scaled[..., :half]], axis=-1)
    return grad * cosine[:, None, :] + back


def mm(a, b):
    return jnp.dot(a, b, preferred_element_type=F32)


def matmul_nt(a, b):
    return lax.dot_general(a, b, (((1,), (1,)), ((), ())), preferred_element_type=F32)


def matmul_tn(a, b):
    return lax.dot_general(a, b, (((0,), (0,)), ((), ())), preferred_element_type=F32)


def swap(v, axis, k):
    n = lax.axis_size(axis)
    return lax.ppermute(v, axis, [(i, i ^ k) for i in range(n)])


def put(buf, v, i):
    return lax.dynamic_update_index_in_dim(buf, v, i, 0)


def take(buf, i):
    return lax.dynamic_index_in_dim(buf, i, 0, keepdims=False)


def gather_slots(v, axis):
    n = lax.axis_size(axis)
    me = lax.axis_index(axis)
    buf = put(jnp.zeros((n, *v.shape), v.dtype), v, me)
    for k in range(1, n):
        buf = put(buf, swap(v, axis, k), me ^ k)
    return buf


def scatter_slots(slots, axis):
    n = lax.axis_size(axis)
    me = lax.axis_index(axis)
    total = take(slots, me).astype(F32)
    for k in range(1, n):
        total = total + swap(take(slots, me ^ k), axis, k).astype(F32)
    return total


def gather_weight(w):
    c = lax.axis_index("core")
    part = gather_slots(gather_slots(w, "zz"), "heads")
    other = swap(part, "core", 1)
    first = jnp.where(c == 0, part, other)
    second = jnp.where(c == 0, other, part)
    return jnp.stack([first, second], axis=2).reshape(-1, w.shape[1])


def scatter_grad(grad):
    nh, nz = lax.axis_size("heads"), lax.axis_size("zz")
    c = lax.axis_index("core")
    n = grad.shape[1]
    g = grad.astype(BF16).reshape(nh, nz, 2, -1, n)
    mine = jnp.where(c == 0, g[:, :, 0], g[:, :, 1])
    theirs = jnp.where(c == 0, g[:, :, 1], g[:, :, 0])
    part = (mine.astype(F32) + swap(theirs, "core", 1).astype(F32)).astype(BF16)
    part = scatter_slots(part, "heads").astype(BF16)
    return scatter_slots(part, "zz")


def all_sum(v):
    for axis in ALL:
        k = 1
        while k < lax.axis_size(axis):
            v = v + swap(v, axis, k)
            k *= 2
    return v


def shards(
    hidden_in,
    segment_ids,
    attn_gain,
    w_query,
    w_key,
    w_value,
    query_gain,
    key_gain,
    w_out,
    ffn_gain,
    w_gate,
    w_up,
    w_down,
    cotangent,
):
    groups, local_len, width = hidden_in.shape
    seq_len = segment_ids.shape[1]
    nh = lax.axis_size("heads")
    h = lax.axis_index("heads")
    nq, nkv = w_query.shape[1], w_key.shape[1]
    q_heads, kv_heads = nq // HD, nkv // HD
    per_kv = q_heads // kv_heads
    ff = w_gate.shape[1] // nh
    shard = w_gate.shape[0]
    scale = HD ** (-0.5)
    longest = seq_len // 4
    nhalo = min(-(-(longest - 1) // local_len), nh - 1)

    w_qkv = gather_weight(jnp.concatenate([w_query, w_key, w_value], axis=1))
    full_o = gather_weight(w_out)

    def column_slices(parts):
        stacked = jnp.concatenate([w.reshape(shard, nh, ff) for w in parts], axis=-1)
        slots = jnp.moveaxis(stacked, 1, 0)
        buf = put(jnp.zeros_like(slots), take(slots, h), h)
        for k in range(1, nh):
            buf = put(buf, swap(take(slots, h ^ k), "heads", k), h ^ k)
        return lax.all_gather(buf, ROWS, axis=1, tiled=True).reshape(width, -1)

    w_gu = column_slices([w_gate, w_up])
    w_dn = column_slices([w_down])

    grad_y = cotangent.reshape(-1, width)
    g_chunks = [grad_y] + [swap(grad_y, "heads", k) for k in range(1, nh)]

    seg = segment_ids.reshape(-1)
    cos_all, sin_all = rotary_tables(positions_of(seg))
    cos = lax.dynamic_slice_in_dim(cos_all, h * local_len, local_len, 0)
    sin = lax.dynamic_slice_in_dim(sin_all, h * local_len, local_len, 0)

    x = hidden_in.astype(F32).reshape(-1, width)
    inv_one = norm_scale(x)
    unit_one = x * inv_one
    normed = (unit_one * attn_gain).astype(BF16)
    qkv = mm(normed, w_qkv)
    q_raw = qkv[:, :nq].reshape(-1, q_heads, HD)
    k_raw = qkv[:, nq : nq + nkv].reshape(-1, kv_heads, HD)
    v_loc = qkv[:, nq + nkv :].astype(BF16)
    q_scale = norm_scale(q_raw)
    q_unit = q_raw * q_scale
    q_rot = rotate(q_unit * query_gain, cos, sin).astype(BF16)
    k_scale = norm_scale(k_raw)
    k_unit = k_raw * k_scale
    k_rot = rotate(k_unit * key_gain, cos, sin).astype(BF16)

    kv = jnp.concatenate([k_rot.reshape(local_len, nkv), v_loc], axis=1)
    pieces = [
        lax.ppermute(kv, "heads", [(i, i + s) for i in range(nh - s)]) for s in range(nhalo, 0, -1)
    ] + [kv]
    kv_ext = jnp.concatenate(pieces, axis=0)
    nkeys = kv_ext.shape[0]
    k_ext = kv_ext[:, :nkv].reshape(nkeys, kv_heads, HD)
    v_ext = kv_ext[:, nkv:].reshape(nkeys, kv_heads, HD)
    seg_pad = jnp.concatenate([jnp.full((nhalo * local_len,), -1, jnp.int32), seg])
    seg_k = lax.dynamic_slice_in_dim(seg_pad, h * local_len, nkeys, 0)
    seg_q = lax.dynamic_slice_in_dim(seg, h * local_len, local_len, 0)
    place_k = jnp.arange(nkeys, dtype=jnp.int32) - nhalo * local_len
    place_q = jnp.arange(local_len, dtype=jnp.int32)
    allowed = (seg_q[:, None] == seg_k[None, :]) & (place_q[:, None] >= place_k[None, :])

    q_g = q_rot.reshape(local_len, kv_heads, per_kv, HD).transpose(1, 2, 0, 3)
    k_g = k_ext.transpose(1, 0, 2)
    v_g = v_ext.transpose(1, 0, 2)
    scores = jnp.einsum("gsqd,gkd->gsqk", q_g, k_g, preferred_element_type=F32) * scale
    scores = jnp.where(allowed[None, None], scores, NEG)
    top = jnp.max(scores, axis=-1, keepdims=True)
    expd = jnp.exp(scores - top)
    total = jnp.sum(expd, axis=-1, keepdims=True)
    probs32 = expd / total
    probs = probs32.astype(BF16)
    mixed_g = jnp.einsum("gsqk,gkd->gsqd", probs, v_g, preferred_element_type=F32).astype(BF16)
    mixed = mixed_g.transpose(2, 0, 1, 3).reshape(local_len, nq)

    resid = x + matmul_nt(mixed, full_o)
    inv_two = norm_scale(resid)
    unit_two = resid * inv_two
    normed_two = (unit_two * ffn_gain).astype(BF16)

    n_chunks = [normed_two] + [swap(normed_two, "heads", k) for k in range(1, nh)]
    outs, backs, d_all = [], [], []
    for k in range(nh):
        gu = mm(n_chunks[k], w_gu)
        gate, up = gu[:, :ff], gu[:, ff:]
        sig = jax.nn.sigmoid(gate)
        act = gate * sig
        hidden = (act * up).astype(BF16)
        d_hidden = mm(g_chunks[k], w_dn)
        d_gate = (d_hidden * up * sig * (1.0 + gate * (1.0 - sig))).astype(BF16)
        d_up = (d_hidden * act).astype(BF16)
        d_gu = jnp.concatenate([d_gate, d_up], axis=1)
        out = matmul_nt(hidden, w_dn)
        back = matmul_nt(d_gu, w_gu)
        if k:
            out = swap(out.astype(BF16), "heads", k).astype(F32)
            back = swap(back.astype(BF16), "heads", k).astype(F32)
        outs.append(out)
        backs.append(back)
        d_all.append((d_gu, hidden))
    layer_out = (resid + sum(outs)).astype(BF16).reshape(groups, local_len, width)
    n_all = jnp.concatenate(n_chunks, axis=0)
    g_all = jnp.concatenate(g_chunks, axis=0)
    d_gu_all = jnp.concatenate([d[0] for d in d_all], axis=0)
    hid_all = jnp.concatenate([d[1] for d in d_all], axis=0)

    def column_grads(grad, count):
        slots = lax.psum_scatter(
            grad.astype(BF16).reshape(nh, -1, count * ff), ROWS, scatter_dimension=1, tiled=True
        )
        buf = put(jnp.zeros_like(slots), take(slots, h), h)
        for k in range(1, nh):
            buf = put(buf, swap(take(slots, h ^ k), "heads", k), h ^ k)
        full = jnp.moveaxis(buf.reshape(nh, shard, count, ff), 2, 0)
        return [full[i].transpose(1, 0, 2).reshape(shard, -1).astype(F32) for i in range(count)]

    (r_down,) = column_grads(matmul_tn(g_all, hid_all), 1)
    r_gate, r_up = column_grads(matmul_tn(n_all, d_gu_all), 2)

    d_normed_two = sum(backs)
    g_ffn = jnp.sum(d_normed_two * unit_two, axis=0)
    d_resid = grad_y.astype(F32) + norm_back(d_normed_two, unit_two, inv_two, ffn_gain)
    d_attn = d_resid.astype(BF16)
    r_out = scatter_grad(matmul_tn(d_attn, mixed))
    d_mixed = mm(d_attn, full_o).astype(BF16)

    d_g = d_mixed.reshape(local_len, kv_heads, per_kv, HD).transpose(1, 2, 0, 3)
    d_probs = jnp.einsum("gsqd,gkd->gsqk", d_g, v_g, preferred_element_type=F32)
    delta = jnp.sum(probs32 * d_probs, axis=-1, keepdims=True)
    d_scores = (probs32 * (d_probs - delta)).astype(BF16)
    d_q = jnp.einsum("gsqk,gkd->gsqd", d_scores, k_g, preferred_element_type=F32) * scale
    d_k = jnp.einsum("gsqk,gsqd->gkd", d_scores, q_g, preferred_element_type=F32) * scale
    d_v = jnp.einsum("gsqk,gsqd->gkd", probs, d_g, preferred_element_type=F32)
    d_kv = jnp.concatenate([d_k, d_v], axis=0).transpose(1, 0, 2).reshape(nkeys, -1)
    d_kv_loc = d_kv[nhalo * local_len :]
    for s in range(1, nhalo + 1):
        lo = (nhalo - s) * local_len
        piece = d_kv[lo : lo + local_len].astype(BF16)
        d_kv_loc = d_kv_loc + lax.ppermute(
            piece, "heads", [(i + s, i) for i in range(nh - s)]
        ).astype(F32)

    d_q_norm = rotate_back(d_q.transpose(2, 0, 1, 3).reshape(local_len, q_heads, HD), cos, sin)
    g_qgain = jnp.sum(d_q_norm * q_unit, axis=(0, 1))
    d_q_raw = norm_back(d_q_norm, q_unit, q_scale, query_gain).astype(BF16).reshape(-1, nq)
    d_k_norm = rotate_back(d_kv_loc[:, :nkv].reshape(-1, kv_heads, HD), cos, sin)
    g_kgain = jnp.sum(d_k_norm * k_unit, axis=(0, 1))
    d_k_raw = norm_back(d_k_norm, k_unit, k_scale, key_gain).astype(BF16).reshape(-1, nkv)
    d_v_raw = d_kv_loc[:, nkv:].astype(BF16)
    d_qkv = jnp.concatenate([d_q_raw, d_k_raw, d_v_raw], axis=1)

    r_qkv = scatter_grad(matmul_tn(normed, d_qkv))
    d_normed = matmul_nt(d_qkv, w_qkv)
    g_attn = jnp.sum(d_normed * unit_one, axis=0)
    grad_in = (
        (d_resid + norm_back(d_normed, unit_one, inv_one, attn_gain))
        .astype(BF16)
        .reshape(groups, local_len, width)
    )
    small = all_sum(jnp.concatenate([g_attn, g_ffn, g_qgain, g_kgain]))
    nz = lax.axis_size("zz")
    at = ((h * nz + lax.axis_index("zz")) * 2 + lax.axis_index("core")) * shard
    r_attn = lax.dynamic_slice_in_dim(small, at, shard, 0)
    r_ffn = lax.dynamic_slice_in_dim(small, width + at, shard, 0)
    return (
        layer_out,
        grad_in,
        r_attn,
        r_qkv[:, :nq],
        r_qkv[:, nq : nq + nkv],
        r_qkv[:, nq + nkv :],
        small[2 * width : 2 * width + HD],
        small[2 * width + HD :],
        r_out,
        r_ffn,
        r_gate,
        r_up,
        r_down,
    )


def solution(mesh):
    nh, nr = mesh.shape["heads"], mesh.shape["rows"]
    fine = Mesh(mesh.devices.reshape(nh, nr // 2, 2), ALL)
    tokens = P(ROWS, "heads", None)
    weight = P(ALL, None)
    vector = P(ALL)
    in_specs = (
        tokens,
        P(ROWS, None),
        P(),
        weight,
        weight,
        weight,
        P(),
        P(),
        weight,
        P(),
        weight,
        weight,
        weight,
        tokens,
    )
    out_specs = (
        tokens,
        tokens,
        vector,
        weight,
        weight,
        weight,
        P(),
        P(),
        weight,
        vector,
        weight,
        weight,
        weight,
    )
    return jax.shard_map(shards, mesh=fine, in_specs=in_specs, out_specs=out_specs, check_vma=False)
```

```python
import math

import jax
import jax.numpy as jnp
from jax import lax
from jax.sharding import Mesh
from jax.sharding import PartitionSpec as P


HD = 64
EPS = 1e-06
NEG = -1e30
THETA = 10000.0
ROWS = ("zz", "core")
ALL = ("heads", "zz", "core")
F32 = jnp.float32
BF16 = jnp.bfloat16


def norm_scale(v):
    return lax.rsqrt(jnp.mean(v * v, axis=-1, keepdims=True) + EPS)


def norm_back(grad_n, unit_v, scale, gain):
    scaled = grad_n * gain
    return scale * (scaled - unit_v * jnp.mean(scaled * unit_v, axis=-1, keepdims=True))


def positions_of(segment_ids):
    places = lax.broadcasted_iota(jnp.int32, segment_ids.shape, 0)
    first = jnp.concatenate(
        [jnp.ones_like(segment_ids[:1]), (segment_ids[1:] != segment_ids[:-1]).astype(jnp.int32)]
    )
    return places - lax.cummax(places * first, axis=0)


def rotary_tables(positions):
    half = HD // 2
    freqs = jnp.exp(jnp.arange(half, dtype=F32) * (-2.0 * math.log(THETA) / HD))
    angles = positions.astype(F32)[:, None] * freqs
    angles = jnp.concatenate([angles, angles], axis=-1)
    return jnp.cos(angles), jnp.sin(angles)


def rotate(v, cosine, sine):
    half = HD // 2
    turned = jnp.concatenate([-v[..., half:], v[..., :half]], axis=-1)
    return v * cosine[:, None, :] + turned * sine[:, None, :]


def rotate_back(grad, cosine, sine):
    half = HD // 2
    scaled = grad * sine[:, None, :]
    back = jnp.concatenate([scaled[..., half:], -scaled[..., :half]], axis=-1)
    return grad * cosine[:, None, :] + back


def mm(a, b):
    return jnp.dot(a, b, preferred_element_type=F32)


def matmul_nt(a, b):
    return lax.dot_general(a, b, (((1,), (1,)), ((), ())), preferred_element_type=F32)


def matmul_tn(a, b):
    return lax.dot_general(a, b, (((0,), (0,)), ((), ())), preferred_element_type=F32)


def swap(v, axis, k):
    n = lax.axis_size(axis)
    return lax.ppermute(v, axis, [(i, i ^ k) for i in range(n)])


def put(buf, v, i):
    return lax.dynamic_update_index_in_dim(buf, v, i, 0)


def take(buf, i):
    return lax.dynamic_index_in_dim(buf, i, 0, keepdims=False)


def everyones(v, axis):
    n = lax.axis_size(axis)
    if axis != "heads" or n != 4:
        return [v] + [swap(v, axis, k) for k in range(1, n)]
    half = v.shape[0] // 2
    one, two = swap(v, axis, 1), swap(v, axis, 2)
    low = swap(one[:half], axis, 2)
    high = swap(two[half:], axis, 1)
    return [v, one, two, jnp.concatenate([low, high], axis=0)]


def settle(got, axis):
    me = lax.axis_index(axis)
    buf = jnp.zeros((len(got), *got[0].shape), got[0].dtype)
    for k, piece in enumerate(got):
        buf = put(buf, piece, me ^ k)
    return buf.reshape(-1, got[0].shape[-1])


def pick_order(got, axis):
    me = lax.axis_index(axis)
    n = len(got)
    out = []
    for j in range(n):
        piece = got[j]
        for i in range(1, n):
            piece = jnp.where(me == i, got[j ^ i], piece)
        out.append(piece)
    return out


def scatter_slots(slots, axis):
    n = lax.axis_size(axis)
    me = lax.axis_index(axis)
    total = take(slots, me).astype(F32)
    parts = [swap(take(slots, me ^ k), axis, k) for k in range(1, n)]
    for part in parts:
        total = total + part.astype(F32)
    return total


def by_core(mine, theirs, axis):
    c = lax.axis_index("core")
    first = jnp.where(c == 0, mine, theirs)
    second = jnp.where(c == 0, theirs, mine)
    return jnp.concatenate([first, second], axis=axis)


def core_cols(v):
    c = lax.axis_index("core")
    half = v.shape[1] // 2
    a, b = v[:, :half], v[:, half:]
    return jnp.where(c == 0, a, b), jnp.where(c == 0, b, a)


def gather_weight(w):
    mine, theirs = core_cols(w)
    got = swap(theirs, "core", 1)
    part = by_core(mine, got, 0)
    part = jnp.concatenate(pick_order(everyones(part, "zz"), "zz"), axis=0)
    parts = everyones(part, "heads")
    others = [swap(p, "core", 1) for p in parts]
    return parts, others


def blocks_of(v):
    n = lax.axis_size("heads")
    size = v.shape[1] // n
    return pick_order([v[:, i * size : (i + 1) * size] for i in range(n)], "heads")


def scatter_grad(mine, theirs):
    nh, nz = lax.axis_size("heads"), lax.axis_size("zz")
    c = lax.axis_index("core")
    n = mine.shape[1]
    other = swap(theirs.astype(BF16), "core", 1)
    part = (mine + other.astype(F32)).astype(BF16).reshape(nh, -1, n)
    part = scatter_slots(part, "heads").astype(BF16)
    part = scatter_slots(part.reshape(nz, -1, n), "zz").reshape(2, -1, n)
    got = swap(take(part, 1 - c).astype(BF16), "core", 1).astype(F32)
    return by_core(take(part, c), got, 1)


def all_sum(v):
    for axis in ALL:
        k = 1
        while k < lax.axis_size(axis):
            other = swap(v, axis, k)
            v = v + other
            k *= 2
    return v


def shards(
    hidden_in,
    segment_ids,
    attn_gain,
    w_query,
    w_key,
    w_value,
    query_gain,
    key_gain,
    w_out,
    ffn_gain,
    w_gate,
    w_up,
    w_down,
    cotangent,
):
    groups, local_len, width = hidden_in.shape
    seq_len = segment_ids.shape[1]
    nh = lax.axis_size("heads")
    h = lax.axis_index("heads")
    nq, nkv = w_query.shape[1], w_key.shape[1]
    q_heads, kv_heads = nq // HD, nkv // HD
    per_kv = q_heads // kv_heads
    ff = w_gate.shape[1] // nh
    shard = w_gate.shape[0]
    scale = HD ** (-0.5)
    longest = seq_len // 4
    nhalo = min(-(-(longest - 1) // local_len), nh - 1)

    def columns_of(at):
        return jnp.concatenate(
            [lax.dynamic_slice_in_dim(w, at * ff, ff, 1) for w in (w_gate, w_up, w_down)], axis=1
        )

    got = [swap(columns_of(h ^ k), "heads", k) for k in range(1, nh)]
    buf = jnp.stack(pick_order([columns_of(h)] + got, "heads"))
    npad = -(nq + 2 * nkv) % 256
    spare = jnp.zeros((shard, npad), BF16)
    qkv_parts, qkv_others = gather_weight(jnp.concatenate([w_query, w_key, w_value, spare], axis=1))
    o_parts, o_others = gather_weight(w_out)
    w_all = lax.all_gather(buf, ROWS, axis=1, tiled=True).reshape(width, -1)
    w_gu, w_dn = w_all[:, : 2 * ff], w_all[:, 2 * ff :]

    grad_y = cotangent.reshape(-1, width)
    g_chunks = everyones(grad_y, "heads")

    seg = segment_ids.reshape(-1)
    cos_all, sin_all = rotary_tables(positions_of(seg))
    cos = lax.dynamic_slice_in_dim(cos_all, h * local_len, local_len, 0)
    sin = lax.dynamic_slice_in_dim(sin_all, h * local_len, local_len, 0)

    x = hidden_in.astype(F32).reshape(-1, width)
    inv_one = norm_scale(x)
    unit_one = x * inv_one
    normed = (unit_one * attn_gain).astype(BF16)
    blocks = blocks_of(normed)
    qkv_mine = sum(mm(b, w) for b, w in zip(blocks, qkv_parts))
    qkv_theirs = sum(mm(b, w) for b, w in zip(blocks, qkv_others))
    qkv = by_core(qkv_mine, qkv_theirs, 1)
    q_raw = qkv[:, :nq].reshape(-1, q_heads, HD)
    k_raw = qkv[:, nq : nq + nkv].reshape(-1, kv_heads, HD)
    v_loc = qkv[:, nq + nkv : nq + 2 * nkv].astype(BF16)
    q_scale = norm_scale(q_raw)
    q_unit = q_raw * q_scale
    q_rot = rotate(q_unit * query_gain, cos, sin).astype(BF16)
    k_scale = norm_scale(k_raw)
    k_unit = k_raw * k_scale
    k_rot = rotate(k_unit * key_gain, cos, sin).astype(BF16)

    kv = jnp.concatenate([k_rot.reshape(local_len, nkv), v_loc], axis=1)
    pieces = [
        lax.ppermute(kv, "heads", [(i, i + s) for i in range(nh - s)])
        for s in range(nhalo, 0, -1)
    ] + [kv]
    kv_ext = jnp.concatenate(pieces, axis=0)
    nkeys = kv_ext.shape[0]
    k_ext = kv_ext[:, :nkv].reshape(nkeys, kv_heads, HD)
    v_ext = kv_ext[:, nkv:].reshape(nkeys, kv_heads, HD)
    seg_pad = jnp.concatenate([jnp.full((nhalo * local_len,), -1, jnp.int32), seg])
    seg_k = lax.dynamic_slice_in_dim(seg_pad, h * local_len, nkeys, 0)
    seg_q = lax.dynamic_slice_in_dim(seg, h * local_len, local_len, 0)
    place_k = jnp.arange(nkeys, dtype=jnp.int32) - nhalo * local_len
    place_q = jnp.arange(local_len, dtype=jnp.int32)
    allowed = (seg_q[:, None] == seg_k[None, :]) & (place_q[:, None] >= place_k[None, :])

    q_g = q_rot.reshape(local_len, kv_heads, per_kv, HD).transpose(1, 2, 0, 3)
    k_g = k_ext.transpose(1, 0, 2)
    v_g = v_ext.transpose(1, 0, 2)
    scores = jnp.einsum("gsqd,gkd->gsqk", q_g, k_g, preferred_element_type=F32) * scale
    scores = jnp.where(allowed[None, None], scores, NEG)
    top = jnp.max(scores, axis=-1, keepdims=True)
    expd = jnp.exp(scores - top)
    total = jnp.sum(expd, axis=-1, keepdims=True)
    probs32 = expd / total
    probs = probs32.astype(BF16)
    mixed_g = jnp.einsum("gsqk,gkd->gsqd", probs, v_g, preferred_element_type=F32).astype(BF16)
    mixed = mixed_g.transpose(2, 0, 1, 3).reshape(local_len, nq)

    mixed_mine, mixed_theirs = core_cols(mixed)
    o_part, o_other = settle(o_parts, "heads"), settle(o_others, "heads")
    attn = matmul_nt(mixed_mine, o_part)
    attn = attn + matmul_nt(mixed_theirs, o_other)
    qkv_part, qkv_other = settle(qkv_parts, "heads"), settle(qkv_others, "heads")
    resid = x + attn
    inv_two = norm_scale(resid)
    unit_two = resid * inv_two
    normed_two = (unit_two * ffn_gain).astype(BF16)

    n_chunks = everyones(normed_two, "heads")
    outs, backs, d_all = [], [], []
    for k in range(nh):
        gu = mm(n_chunks[k], w_gu)
        gate, up = gu[:, :ff], gu[:, ff:]
        sig = jax.nn.sigmoid(gate)
        act = gate * sig
        hidden = (act * up).astype(BF16)
        d_hidden = mm(g_chunks[k], w_dn)
        d_gate = (d_hidden * up * sig * (1.0 + gate * (1.0 - sig))).astype(BF16)
        d_up = (d_hidden * act).astype(BF16)
        d_gu = jnp.concatenate([d_gate, d_up], axis=1)
        back = matmul_nt(d_gu, w_gu)
        if k:
            back = swap(back.astype(BF16), "heads", k)
            back = back.astype(F32)
        out = matmul_nt(hidden, w_dn)
        if k:
            out = swap(out.astype(BF16), "heads", k)
            out = out.astype(F32)
        outs.append(out)
        backs.append(back)
        d_all.append((d_gu, hidden))
    layer_out = (resid + sum(outs)).astype(BF16).reshape(groups, local_len, width)
    n_all = jnp.concatenate(n_chunks, axis=0)
    g_all = jnp.concatenate(g_chunks, axis=0)
    d_gu_all = jnp.concatenate([d[0] for d in d_all], axis=0)
    hid_all = jnp.concatenate([d[1] for d in d_all], axis=0)

    def column_grads(grad, count):
        slots = lax.psum_scatter(
            grad.astype(BF16).reshape(nh, -1, count * ff), ROWS, scatter_dimension=1, tiled=True
        )
        got = [swap(take(slots, h ^ k), "heads", k) for k in range(1, nh)]
        full = pick_order([take(slots, h)] + got, "heads")
        return [
            jnp.concatenate([p[:, i * ff : (i + 1) * ff] for p in full], axis=1).astype(F32)
            for i in range(count)
        ]

    grad_dn = matmul_tn(g_all, hid_all)
    grad_gu = matmul_tn(n_all, d_gu_all).astype(BF16)
    (r_down,) = column_grads(grad_dn, 1)
    r_gate, r_up = column_grads(grad_gu, 2)

    d_normed_two = sum(backs)
    g_ffn = jnp.sum(d_normed_two * unit_two, axis=0)
    d_resid = grad_y.astype(F32) + norm_back(d_normed_two, unit_two, inv_two, ffn_gain)
    d_attn = d_resid.astype(BF16)
    go_theirs = matmul_tn(d_attn, mixed_theirs)
    go_mine = matmul_tn(d_attn, mixed_mine)
    r_out = scatter_grad(go_mine, go_theirs)
    d_mixed_mine = mm(d_attn, o_part).astype(BF16)
    d_mixed_theirs = mm(d_attn, o_other).astype(BF16)
    d_mixed = by_core(d_mixed_mine, d_mixed_theirs, 1)

    d_g = d_mixed.reshape(local_len, kv_heads, per_kv, HD).transpose(1, 2, 0, 3)
    d_probs = jnp.einsum("gsqd,gkd->gsqk", d_g, v_g, preferred_element_type=F32)
    delta = jnp.sum(probs32 * d_probs, axis=-1, keepdims=True)
    d_scores = (probs32 * (d_probs - delta)).astype(BF16)
    d_q = jnp.einsum("gsqk,gkd->gsqd", d_scores, k_g, preferred_element_type=F32) * scale
    d_k = jnp.einsum("gsqk,gsqd->gkd", d_scores, q_g, preferred_element_type=F32) * scale
    d_v = jnp.einsum("gsqk,gsqd->gkd", probs, d_g, preferred_element_type=F32)
    d_kv = jnp.concatenate([d_k, d_v], axis=0).transpose(1, 0, 2).reshape(nkeys, -1)
    d_kv_loc = d_kv[nhalo * local_len :]
    for s in range(1, nhalo + 1):
        lo = (nhalo - s) * local_len
        piece = d_kv[lo : lo + local_len].astype(BF16)
        d_kv_loc = d_kv_loc + lax.ppermute(
            piece, "heads", [(i + s, i) for i in range(nh - s)]
        ).astype(F32)

    d_q_norm = rotate_back(d_q.transpose(2, 0, 1, 3).reshape(local_len, q_heads, HD), cos, sin)
    g_qgain = jnp.sum(d_q_norm * q_unit, axis=(0, 1))
    d_q_raw = norm_back(d_q_norm, q_unit, q_scale, query_gain).astype(BF16).reshape(-1, nq)
    d_k_norm = rotate_back(d_kv_loc[:, :nkv].reshape(-1, kv_heads, HD), cos, sin)
    g_kgain = jnp.sum(d_k_norm * k_unit, axis=(0, 1))
    d_k_raw = norm_back(d_k_norm, k_unit, k_scale, key_gain).astype(BF16).reshape(-1, nkv)
    d_v_raw = d_kv_loc[:, nkv:].astype(BF16)
    spare = jnp.zeros((local_len, npad), BF16)
    d_mine, d_theirs = core_cols(jnp.concatenate([d_q_raw, d_k_raw, d_v_raw, spare], axis=1))
    gq_theirs = matmul_tn(normed, d_theirs)
    gq_mine = matmul_tn(normed, d_mine)
    r_qkv = scatter_grad(gq_mine, gq_theirs)
    d_normed = matmul_nt(d_mine, qkv_part)
    d_normed = d_normed + matmul_nt(d_theirs, qkv_other)
    g_attn = jnp.sum(d_normed * unit_one, axis=0)
    grad_in = (
        (d_resid + norm_back(d_normed, unit_one, inv_one, attn_gain))
        .astype(BF16)
        .reshape(groups, local_len, width)
    )
    small = all_sum(jnp.concatenate([g_attn, g_ffn, g_qgain, g_kgain]))
    nz = lax.axis_size("zz")
    at = ((h * nz + lax.axis_index("zz")) * 2 + lax.axis_index("core")) * shard
    r_attn = lax.dynamic_slice_in_dim(small, at, shard, 0)
    r_ffn = lax.dynamic_slice_in_dim(small, width + at, shard, 0)
    return (
        layer_out,
        grad_in,
        r_attn,
        r_qkv[:, :nq],
        r_qkv[:, nq : nq + nkv],
        r_qkv[:, nq + nkv : nq + 2 * nkv],
        small[2 * width : 2 * width + HD],
        small[2 * width + HD :],
        r_out,
        r_ffn,
        r_gate,
        r_up,
        r_down,
    )


def solution(mesh):
    nh, nr = mesh.shape["heads"], mesh.shape["rows"]
    fine = Mesh(mesh.devices.reshape(nh, nr // 2, 2), ALL)
    tokens = P(ROWS, "heads", None)
    weight = P(ALL, None)
    vector = P(ALL)
    in_specs = (
        tokens,
        P(ROWS, None),
        P(),
        weight,
        weight,
        weight,
        P(),
        P(),
        weight,
        P(),
        weight,
        weight,
        weight,
        tokens,
    )
    out_specs = (
        tokens,
        tokens,
        vector,
        weight,
        weight,
        weight,
        P(),
        P(),
        weight,
        vector,
        weight,
        weight,
        weight,
    )

    return jax.shard_map(shards, mesh=fine, in_specs=in_specs, out_specs=out_specs, check_vma=False)
```

```python
import functools
import math

import jax
import jax.numpy as jnp
from jax import lax
from jax.experimental import pallas as pl
from jax.experimental.pallas import tpu as pltpu
from jax.sharding import Mesh
from jax.sharding import PartitionSpec as P


HEADS, ZZ, CORE = "heads", "zz", "core"

HD = 64
PAIR = 2 * HD
EPS = 1e-06
NEG = -1e30
THETA = 10000.0
ROWS = (ZZ, CORE)
ALL = (HEADS, ZZ, CORE)
F32 = jnp.float32
BF16 = jnp.bfloat16


def norm_scale(v):
    return lax.rsqrt(jnp.mean(v * v, axis=-1, keepdims=True) + EPS)


def norm_back(grad_n, unit_v, scale, gain):
    scaled = grad_n * gain
    return scale * (scaled - unit_v * jnp.mean(scaled * unit_v, axis=-1, keepdims=True))


def positions_of(segment_ids):
    places = lax.broadcasted_iota(jnp.int32, segment_ids.shape, 0)
    first = jnp.concatenate(
        [jnp.ones_like(segment_ids[:1]), (segment_ids[1:] != segment_ids[:-1]).astype(jnp.int32)]
    )
    return places - lax.cummax(places * first, axis=0)


def rotary_tables(positions):
    half = HD // 2
    freqs = jnp.exp(jnp.arange(half, dtype=F32) * (-2.0 * math.log(THETA) / HD))
    angles = positions.astype(F32)[:, None] * freqs
    angles = jnp.concatenate([angles, angles], axis=-1)
    sign = jnp.where(jnp.arange(HD) < half, -1.0, 1.0)
    return jnp.tile(jnp.cos(angles), (1, 2)), jnp.tile(jnp.sin(angles) * sign, (1, 2))


def mm(a, b):
    return jnp.dot(a, b, preferred_element_type=F32)


def swap(v, axis, k):
    n = lax.axis_size(axis)
    return lax.ppermute(v, axis, [(i, i ^ k) for i in range(n)])


def put(buf, v, i):
    return lax.dynamic_update_index_in_dim(buf, v, i, 0)


def take(buf, i):
    return lax.dynamic_index_in_dim(buf, i, 0, keepdims=False)


def everyones(v, axis):
    n = lax.axis_size(axis)
    if axis != HEADS or n != 4:
        return [v] + [swap(v, axis, k) for k in range(1, n)]
    half = v.shape[0] // 2
    one, two = swap(v, axis, 1), swap(v, axis, 2)
    low = swap(one[:half], axis, 2)
    high = swap(two[half:], axis, 1)
    return [v, one, two, jnp.concatenate([low, high], axis=0)]


def settle(got, axis):
    me = lax.axis_index(axis)
    buf = jnp.zeros((len(got), *got[0].shape), got[0].dtype)
    for k, piece in enumerate(got):
        buf = put(buf, piece, me ^ k)
    return buf.reshape(-1, got[0].shape[-1])


def pick_order(got, axis):
    me = lax.axis_index(axis)
    n = len(got)
    out = []
    for j in range(n):
        piece = got[j]
        for i in range(1, n):
            piece = jnp.where(me == i, got[j ^ i], piece)
        out.append(piece)
    return out


def scatter_slots(slots, axis, dtype):
    n = lax.axis_size(axis)
    me = lax.axis_index(axis)
    total = take(slots, me).astype(F32)
    parts = [swap(take(slots, me ^ k), axis, k) for k in range(1, n)]
    for part in parts:
        total = total + part.astype(F32)
    return total.astype(dtype)


def by_core(mine, theirs, axis):
    c = lax.axis_index(CORE)
    first = jnp.where(c == 0, mine, theirs)
    second = jnp.where(c == 0, theirs, mine)
    return jnp.concatenate([first, second], axis=axis)


def core_cols(v):
    c = lax.axis_index(CORE)
    half = v.shape[1] // 2
    a, b = v[:, :half], v[:, half:]
    return jnp.where(c == 0, a, b), jnp.where(c == 0, b, a)


def gather_weight(w):
    mine, theirs = core_cols(w)
    got = swap(theirs, CORE, 1)
    part = by_core(mine, got, 0)
    got = everyones(part, ZZ)
    part = jnp.concatenate(pick_order(got, ZZ), axis=0)
    parts = everyones(part, HEADS)
    others = [swap(p, CORE, 1) for p in parts]
    return parts, others


def blocks_of(v):
    n = lax.axis_size(HEADS)
    size = v.shape[1] // n
    return pick_order([v[:, i * size : (i + 1) * size] for i in range(n)], HEADS)


def scatter_grad(mine, theirs):
    nh, nz = lax.axis_size(HEADS), lax.axis_size(ZZ)
    c = lax.axis_index(CORE)
    n = mine.shape[1]
    other = swap(theirs.astype(BF16), CORE, 1)
    part = (mine + other.astype(F32)).astype(BF16).reshape(nh, -1, n)
    part = scatter_slots(part, HEADS, BF16)
    part = scatter_slots(part.reshape(nz, -1, n), ZZ, F32).reshape(2, -1, n)
    got = swap(take(part, 1 - c).astype(BF16), CORE, 1).astype(F32)
    return by_core(take(part, c), got, 1)


def all_sum(v):
    for axis in (CORE, ZZ, HEADS):
        k = 1
        while k < lax.axis_size(axis):
            other = swap(v, axis, k)
            v = v + other
            k *= 2
    return v


def pair_norm(x, first):
    sq = x * x
    low = jnp.sum(jnp.where(first, sq, 0.0), axis=-1, keepdims=True)
    high = jnp.sum(jnp.where(first, 0.0, sq), axis=-1, keepdims=True)
    return lax.rsqrt(jnp.where(first, low, high) * (1.0 / HD) + EPS)


def pair_mean(x, first):
    low = jnp.sum(jnp.where(first, x, 0.0), axis=-1, keepdims=True)
    high = jnp.sum(jnp.where(first, 0.0, x), axis=-1, keepdims=True)
    return jnp.where(first, low, high) * (1.0 / HD)


def half_turn(x, early):
    return jnp.where(early, pltpu.roll(x, PAIR - HD // 2, 1), pltpu.roll(x, HD // 2, 1))


def lane_masks(rows):
    lane = lax.broadcasted_iota(jnp.int32, (rows, PAIR), 1)
    return lane < HD, (lane % HD) < HD // 2


def rotate_kernel(qk_ref, cos_ref, sin_ref, gain_ref, q_ref, kv_ref, *, nrot, scale):
    first, early = lane_masks(qk_ref.shape[0])
    cos, sin = cos_ref[...], sin_ref[...]
    nq = q_ref.shape[1]
    cols = nq + kv_ref.shape[1]
    for p in range(cols // PAIR):
        at = slice(p * PAIR, (p + 1) * PAIR)
        x = qk_ref[:, at]
        live = min(max(nrot - 2 * p, 0), 2)
        if live:
            a = x * pair_norm(x, first) * gain_ref[:, at]
            y = a * cos + half_turn(a, early) * sin
            x = y if live == 2 else jnp.where(first, y, x)
        if p * PAIR < nq:
            q_ref[:, at] = (x * scale).astype(BF16)
        else:
            kv_ref[:, p * PAIR - nq : (p + 1) * PAIR - nq] = x.astype(BF16)


def unrotate_kernel(d_ref, x_ref, cos_ref, sin_ref, gain_ref, out_ref, dgain_ref, *, nrot, start):
    first, early = lane_masks(d_ref.shape[0])
    cos, sin = cos_ref[...], sin_ref[...]
    total = jnp.zeros((1, PAIR), F32)
    for p in range(d_ref.shape[1] // PAIR):
        at = slice(p * PAIR, (p + 1) * PAIR)
        d = d_ref[:, at]
        live = min(max(nrot - 2 * p, 0), 2)
        if live:
            there = slice(start + p * PAIR, start + (p + 1) * PAIR)
            x = x_ref[:, there]
            scale = pair_norm(x, first)
            unit = x * scale
            da = d * cos + half_turn(d * sin, early)
            if live == 1:
                da = jnp.where(first, da, 0.0)
            total = total + jnp.sum(da * unit, axis=0, keepdims=True)
            n = da * gain_ref[:, there]
            y = scale * (n - unit * pair_mean(n * unit, first))
            d = y if live == 2 else jnp.where(first, y, d)
        out_ref[:, at] = d.astype(BF16)
    dgain_ref[...] = total


def dot_nt(a, b):
    return lax.dot_general(a, b, (((1,), (1,)), ((), ())), preferred_element_type=F32)


def dot_tn(a, b):
    return lax.dot_general(a, b, (((0,), (0,)), ((), ())), preferred_element_type=F32)


def head_rows(ref, rows, g, per):
    return jnp.concatenate(
        [ref[rows, (g * per + i) * HD : (g * per + i + 1) * HD] for i in range(per)], axis=0
    )


def head_lanes(v, per):
    size = v.shape[0] // per
    return jnp.concatenate([v[i * size : (i + 1) * size] for i in range(per)], axis=1)


def attend_kernel(q_ref, kv_ref, segq_ref, segk_ref, out_ref, *, kvh, per, block):
    rows, keys = q_ref.shape[0], kv_ref.shape[0]
    band = keys - rows + block
    for lo in range(0, rows, block):
        at, near = slice(lo, lo + block), slice(lo, lo + band)
        place_q = lax.broadcasted_iota(jnp.int32, (block, band), 0) + (keys - rows)
        place_k = lax.broadcasted_iota(jnp.int32, (block, band), 1)
        bias = jnp.where(
            (segq_ref[at, :] == segk_ref[:, near]) & (place_q >= place_k), 0.0, NEG
        )
        for g in range(kvh):
            k = kv_ref[near, g * HD : (g + 1) * HD]
            v = kv_ref[near, (kvh + g) * HD : (kvh + g + 1) * HD]
            s = dot_nt(head_rows(q_ref, at, g, per), k)
            s = s.reshape(per, block, band) + bias[None]
            e = jnp.exp(s - jnp.max(s, axis=-1, keepdims=True))
            p = e * (1.0 / jnp.sum(e, axis=-1, keepdims=True))
            o = jnp.dot(
                p.astype(BF16).reshape(per * block, band), v, preferred_element_type=F32
            )
            out_ref[at, g * per * HD : (g + 1) * per * HD] = head_lanes(o, per).astype(BF16)


def attend_back_kernel(
    q_ref, kv_ref, d_ref, segq_ref, segk_ref, dq_ref, dkv_ref, *, kvh, per, block, scale
):
    rows, keys = q_ref.shape[0], kv_ref.shape[0]
    band = keys - rows + block
    dkv_ref[...] = jnp.zeros_like(dkv_ref)
    for lo in range(0, rows, block):
        at, near = slice(lo, lo + block), slice(lo, lo + band)
        place_k = lax.broadcasted_iota(jnp.int32, (band, block), 0)
        place_q = lax.broadcasted_iota(jnp.int32, (band, block), 1) + (keys - rows)
        bias = jnp.where(
            (segk_ref[near, :] == segq_ref[:, at]) & (place_q >= place_k), 0.0, NEG
        )
        bias = jnp.concatenate([bias] * per, axis=1)
        for g in range(kvh):
            ks = slice(g * HD, (g + 1) * HD)
            vs = slice((kvh + g) * HD, (kvh + g + 1) * HD)
            k, v = kv_ref[near, ks], kv_ref[near, vs]
            q, d = head_rows(q_ref, at, g, per), head_rows(d_ref, at, g, per)
            s = dot_nt(k, q) + bias
            e = jnp.exp(s - jnp.max(s, axis=0, keepdims=True))
            p = e * (1.0 / jnp.sum(e, axis=0, keepdims=True))
            dp = dot_nt(v, d)
            delta = jnp.sum(p * dp, axis=0, keepdims=True)
            ds = (p * (dp - delta)).astype(BF16)
            dkv_ref[near, ks] += jnp.dot(ds, q, preferred_element_type=F32)
            dkv_ref[near, vs] += jnp.dot(p.astype(BF16), d, preferred_element_type=F32)
            dq = dot_tn(ds, k) * scale
            dq_ref[at, g * per * HD : (g + 1) * per * HD] = head_lanes(dq, per)


def weight_grad_kernel(*refs, chunks, parts):
    lefts, rights, out_ref = refs[:chunks], refs[chunks:-1], refs[-1]
    size = rights[0].shape[1]
    for i in range(parts):
        total = sum(
            dot_tn(left[...], rights[k * parts + i][...]) for k, left in enumerate(lefts)
        )
        out_ref[:, i * size : (i + 1) * size] = total.astype(BF16)


def weight_grad(lefts, rights):
    chunks, parts = len(lefts), len(rights[0])
    rows, width = lefts[0].shape
    size = rights[0][0].shape[1]
    block = min(width, 256)
    right_spec = pl.BlockSpec((rows, size), lambda i: (0, 0))
    return pl.pallas_call(
        functools.partial(weight_grad_kernel, chunks=chunks, parts=parts),
        grid=(width // block,),
        in_specs=[pl.BlockSpec((rows, block), lambda i: (0, i))] * chunks
        + [right_spec] * (chunks * parts),
        out_specs=pl.BlockSpec((block, parts * size), lambda i: (i, 0)),
        out_shape=jax.ShapeDtypeStruct((width, parts * size), BF16),
        compiler_params=pltpu.CompilerParams(vmem_limit_bytes=48 << 20),
    )(*lefts, *[r for row in rights for r in row])


def local_call(kernel, outs, *args):
    return pl.pallas_call(
        kernel,
        out_shape=[jax.ShapeDtypeStruct(shape, dtype) for shape, dtype in outs],
        compiler_params=pltpu.CompilerParams(vmem_limit_bytes=48 << 20),
    )(*args)


def shards(
    hidden_in,
    segment_ids,
    attn_gain,
    w_query,
    w_key,
    w_value,
    query_gain,
    key_gain,
    w_out,
    ffn_gain,
    w_gate,
    w_up,
    w_down,
    cotangent,
):
    groups, local_len, width = hidden_in.shape
    seq_len = segment_ids.shape[1]
    nh = lax.axis_size(HEADS)
    h = lax.axis_index(HEADS)
    nq, nkv = w_query.shape[1], w_key.shape[1]
    q_heads, kv_heads = nq // HD, nkv // HD
    per_kv = q_heads // kv_heads
    ff = w_gate.shape[1] // nh
    shard = w_gate.shape[0]
    scale = HD ** (-0.5)
    longest = seq_len // 4
    nhalo = min(-(-(longest - 1) // local_len), nh - 1)

    def columns_of(at):
        return jnp.concatenate(
            [lax.dynamic_slice_in_dim(w, at * ff, ff, 1) for w in (w_gate, w_up, w_down)], axis=1
        )

    got = [swap(columns_of(h ^ k), HEADS, k) for k in range(1, nh)]
    buf = jnp.stack(pick_order([columns_of(h)] + got, HEADS))
    npad = -(nq + 2 * nkv) % 256
    spare = jnp.zeros((shard, npad), BF16)
    qkv_parts, qkv_others = gather_weight(jnp.concatenate([w_query, w_key, w_value, spare], axis=1))
    o_parts, o_others = gather_weight(w_out)
    w_all = lax.all_gather(buf, ROWS, axis=1, tiled=True).reshape(width, -1)
    w_gu, w_dn = w_all[:, : 2 * ff], w_all[:, 2 * ff :]

    grad_y = cotangent.reshape(-1, width)
    g_chunks = everyones(grad_y, HEADS)

    seg = segment_ids.reshape(-1)
    mine = lax.dynamic_slice_in_dim(positions_of(seg), h * local_len, local_len, 0)
    cos, sin = rotary_tables(mine)

    x = hidden_in.astype(F32).reshape(-1, width)
    inv_one = norm_scale(x)
    unit_one = x * inv_one
    normed = (unit_one * attn_gain).astype(BF16)
    blocks = blocks_of(normed)
    qkv_mine = sum(mm(b, w) for b, w in zip(blocks, qkv_parts))
    qkv_theirs = sum(mm(b, w) for b, w in zip(blocks, qkv_others))
    qkv = by_core(qkv_mine, qkv_theirs, 1)
    gains = jnp.concatenate(
        [
            jnp.tile(query_gain, q_heads),
            jnp.tile(key_gain, kv_heads),
            jnp.zeros((nkv,), F32),
        ]
    )[None]
    q_rot, kv = local_call(
        functools.partial(rotate_kernel, nrot=q_heads + kv_heads, scale=scale),
        [((local_len, nq), BF16), ((local_len, 2 * nkv), BF16)],
        qkv,
        cos,
        sin,
        gains,
    )
    pieces = [
        lax.ppermute(kv, HEADS, [(i, i + s) for i in range(nh - s)])
        for s in range(nhalo, 0, -1)
    ] + [kv]
    kv_ext = jnp.concatenate(pieces, axis=0)
    nkeys = kv_ext.shape[0]
    seg_pad = jnp.concatenate([jnp.full((nhalo * local_len,), -1, jnp.int32), seg])
    seg_k = lax.dynamic_slice_in_dim(seg_pad, h * local_len, nkeys, 0)
    seg_q = lax.dynamic_slice_in_dim(seg, h * local_len, local_len, 0)
    shape = dict(kvh=kv_heads, per=per_kv, block=min(local_len, 128))
    (mixed,) = local_call(
        functools.partial(attend_kernel, **shape),
        [((local_len, nq), BF16)],
        q_rot,
        kv_ext,
        seg_q[:, None],
        seg_k[None],
    )
    mixed_mine, mixed_theirs = core_cols(mixed)
    attn = [
        dot_nt(mixed_mine, p) + dot_nt(mixed_theirs, q) for p, q in zip(o_parts, o_others)
    ]
    attn = jnp.concatenate(pick_order(attn, HEADS), axis=1)
    resid = x + attn
    inv_two = norm_scale(resid)
    unit_two = resid * inv_two
    normed_two = (unit_two * ffn_gain).astype(BF16)

    o_part, o_other = settle(o_parts, HEADS), settle(o_others, HEADS)
    qkv_part, qkv_other = settle(qkv_parts, HEADS), settle(qkv_others, HEADS)
    n_chunks = everyones(normed_two, HEADS)
    outs, backs, d_all = [], [], []
    for k in range(nh):
        gu = mm(n_chunks[k], w_gu)
        gate, up = gu[:, :ff], gu[:, ff:]
        sig = jax.nn.sigmoid(gate)
        act = gate * sig
        hidden = (act * up).astype(BF16)
        d_hidden = mm(g_chunks[k], w_dn)
        d_gate = (d_hidden * up * sig * (1.0 + gate * (1.0 - sig))).astype(BF16)
        d_up = (d_hidden * act).astype(BF16)
        d_gu = jnp.concatenate([d_gate, d_up], axis=1)
        back = dot_nt(d_gu, w_gu)
        if k:
            back = swap(back.astype(BF16), HEADS, k)
            back = back.astype(F32)
        out = dot_nt(hidden, w_dn)
        if k:
            out = swap(out.astype(BF16), HEADS, k)
            out = out.astype(F32)
        outs.append(out)
        backs.append(back)
        d_all.append(([d_gate, d_up], [hidden]))
    layer_out = (resid + sum(outs)).astype(BF16).reshape(groups, local_len, width)

    def column_grads(grad, count):
        slots = lax.psum_scatter(
            grad.reshape(nh, -1, count * ff), ROWS, scatter_dimension=1, tiled=True
        )
        got = [swap(take(slots, h ^ k), HEADS, k) for k in range(1, nh)]
        full = pick_order([take(slots, h)] + got, HEADS)
        return [
            jnp.concatenate([p[:, i * ff : (i + 1) * ff] for p in full], axis=1).astype(F32)
            for i in range(count)
        ]

    grad_dn = weight_grad(g_chunks, [d[1] for d in d_all])
    grad_gu = weight_grad(n_chunks, [d[0] for d in d_all])
    (r_down,) = column_grads(grad_dn, 1)
    r_gate, r_up = column_grads(grad_gu, 2)

    d_normed_two = sum(backs)
    g_ffn = jnp.sum(d_normed_two * unit_two, axis=0)
    d_resid = grad_y.astype(F32) + norm_back(d_normed_two, unit_two, inv_two, ffn_gain)
    d_attn = d_resid.astype(BF16)
    go_theirs = dot_tn(d_attn, mixed_theirs)
    go_mine = dot_tn(d_attn, mixed_mine)
    r_out = scatter_grad(go_mine, go_theirs)
    d_mixed_mine = mm(d_attn, o_part).astype(BF16)
    d_mixed_theirs = mm(d_attn, o_other).astype(BF16)
    d_mixed = by_core(d_mixed_mine, d_mixed_theirs, 1)

    d_q, d_kv = local_call(
        functools.partial(attend_back_kernel, scale=scale, **shape),
        [((local_len, nq), F32), ((nkeys, 2 * nkv), F32)],
        q_rot,
        kv_ext,
        d_mixed,
        seg_q[None],
        seg_k[:, None],
    )
    d_kv_loc = d_kv[nhalo * local_len :]
    for s in range(1, nhalo + 1):
        lo = (nhalo - s) * local_len
        piece = d_kv[lo : lo + local_len].astype(BF16)
        piece = lax.ppermute(piece, HEADS, [(i + s, i) for i in range(nh - s)])
        d_kv_loc = d_kv_loc + piece.astype(F32)

    def unrotate(d, nrot, start):
        return local_call(
            functools.partial(unrotate_kernel, nrot=nrot, start=start),
            [(d.shape, BF16), ((1, PAIR), F32)],
            d,
            qkv,
            cos,
            sin,
            gains,
        )

    d_q_raw, g_qgain = unrotate(d_q, q_heads, 0)
    d_kv_raw, g_kgain = unrotate(d_kv_loc, kv_heads, nq)
    g_qgain = g_qgain[0, :HD] + g_qgain[0, HD:]
    g_kgain = g_kgain[0, :HD] + g_kgain[0, HD:]
    spare = jnp.zeros((local_len, npad), BF16)
    d_mine, d_theirs = core_cols(jnp.concatenate([d_q_raw, d_kv_raw, spare], axis=1))
    gq_theirs = dot_tn(normed, d_theirs)
    gq_mine = dot_tn(normed, d_mine)
    r_qkv = scatter_grad(gq_mine, gq_theirs)
    d_normed = dot_nt(d_mine, qkv_part)
    d_normed = d_normed + dot_nt(d_theirs, qkv_other)
    g_attn = jnp.sum(d_normed * unit_one, axis=0)
    grad_in = (
        (d_resid + norm_back(d_normed, unit_one, inv_one, attn_gain))
        .astype(BF16)
        .reshape(groups, local_len, width)
    )
    small = all_sum(jnp.concatenate([g_attn, g_ffn, g_qgain, g_kgain]))
    nz = lax.axis_size(ZZ)
    at = ((h * nz + lax.axis_index(ZZ)) * 2 + lax.axis_index(CORE)) * shard
    r_attn = lax.dynamic_slice_in_dim(small, at, shard, 0)
    r_ffn = lax.dynamic_slice_in_dim(small, width + at, shard, 0)
    return (
        layer_out,
        grad_in,
        r_attn,
        r_qkv[:, :nq],
        r_qkv[:, nq : nq + nkv],
        r_qkv[:, nq + nkv : nq + 2 * nkv],
        small[2 * width : 2 * width + HD],
        small[2 * width + HD :],
        r_out,
        r_ffn,
        r_gate,
        r_up,
        r_down,
    )


def solution(mesh):
    nh, nr = mesh.shape[HEADS], mesh.shape["rows"]
    fine = Mesh(mesh.devices.reshape(nh, nr // 2, 2), ALL)
    tokens = P(ROWS, HEADS, None)
    weight = P(ALL, None)
    vector = P(ALL)
    in_specs = (
        tokens,
        P(ROWS, None),
        P(),
        weight,
        weight,
        weight,
        P(),
        P(),
        weight,
        P(),
        weight,
        weight,
        weight,
        tokens,
    )
    out_specs = (
        tokens,
        tokens,
        vector,
        weight,
        weight,
        weight,
        P(),
        P(),
        weight,
        vector,
        weight,
        weight,
        weight,
    )

    return jax.shard_map(shards, mesh=fine, in_specs=in_specs, out_specs=out_specs, check_vma=False)
```

```python
import functools
import math

import jax
import jax.numpy as jnp
from jax import lax
from jax.experimental import pallas as pl
from jax.experimental.pallas import tpu as pltpu
from jax.sharding import Mesh
from jax.sharding import PartitionSpec as P


HEADS, ZZ, CORE = "heads", "zz", "core"

HD = 64
PAIR = 2 * HD
EPS = 1e-06
NEG = -1e30
THETA = 10000.0
ROWS = (ZZ, CORE)
ALL = (HEADS, ZZ, CORE)
F32 = jnp.float32
BF16 = jnp.bfloat16


def norm_scale(v):
    return lax.rsqrt(jnp.mean(v * v, axis=-1, keepdims=True) + EPS)


def norm_back(grad_n, unit_v, scale, gain):
    scaled = grad_n * gain
    return scale * (scaled - unit_v * jnp.mean(scaled * unit_v, axis=-1, keepdims=True))


def positions_of(segment_ids):
    places = lax.broadcasted_iota(jnp.int32, segment_ids.shape, 0)
    first = jnp.concatenate(
        [jnp.ones_like(segment_ids[:1]), (segment_ids[1:] != segment_ids[:-1]).astype(jnp.int32)]
    )
    return places - lax.cummax(places * first, axis=0)


def rotary_tables(positions):
    half = HD // 2
    freqs = jnp.exp(jnp.arange(half, dtype=F32) * (-2.0 * math.log(THETA) / HD))
    angles = positions.astype(F32)[:, None] * freqs
    angles = jnp.concatenate([angles, angles], axis=-1)
    sign = jnp.where(jnp.arange(HD) < half, -1.0, 1.0)
    return jnp.tile(jnp.cos(angles), (1, 2)), jnp.tile(jnp.sin(angles) * sign, (1, 2))


def mm(a, b):
    return jnp.dot(a, b, preferred_element_type=F32)


def swap(v, axis, k):
    n = lax.axis_size(axis)
    return lax.ppermute(v, axis, [(i, i ^ k) for i in range(n)])


def put(buf, v, i):
    return lax.dynamic_update_index_in_dim(buf, v, i, 0)


def take(buf, i):
    return lax.dynamic_index_in_dim(buf, i, 0, keepdims=False)


def everyones(v, axis):
    n = lax.axis_size(axis)
    if axis != HEADS or n != 4:
        return [v] + [swap(v, axis, k) for k in range(1, n)]
    half = v.shape[0] // 2
    one, two = swap(v, axis, 1), swap(v, axis, 2)
    low = swap(one[:half], axis, 2)
    high = swap(two[half:], axis, 1)
    return [v, one, two, jnp.concatenate([low, high], axis=0)]


def settle(got, axis):
    me = lax.axis_index(axis)
    buf = jnp.zeros((len(got), *got[0].shape), got[0].dtype)
    for k, piece in enumerate(got):
        buf = put(buf, piece, me ^ k)
    return buf.reshape(-1, got[0].shape[-1])


def fold(parts, dtype):
    n = len(parts)
    if n != 4:
        got = [swap(p.astype(BF16), HEADS, k) for k, p in enumerate(parts) if k]
        return sum((g.astype(F32) for g in got), parts[0].astype(F32)).astype(dtype)
    half = parts[0].shape[0] // 2
    low, high = [p[:half] for p in parts], [p[half:] for p in parts]
    one = swap(jnp.stack([low[1], low[3]]).astype(BF16), HEADS, 1)
    two = swap(jnp.stack([high[2], high[3]]).astype(BF16), HEADS, 2)
    low_on = (low[2].astype(F32) + one[1].astype(F32)).astype(BF16)
    high_on = (high[1].astype(F32) + two[1].astype(F32)).astype(BF16)
    low_end = swap(low_on, HEADS, 2)
    high_end = swap(high_on, HEADS, 1)
    low_sum = low[0].astype(F32) + one[0].astype(F32) + low_end.astype(F32)
    high_sum = high[0].astype(F32) + two[0].astype(F32) + high_end.astype(F32)
    return jnp.concatenate([low_sum, high_sum], axis=0).astype(dtype)


def pick_order(got, axis):
    me = lax.axis_index(axis)
    n = len(got)
    out = []
    for j in range(n):
        piece = got[j]
        for i in range(1, n):
            piece = jnp.where(me == i, got[j ^ i], piece)
        out.append(piece)
    return out


def scatter_slots(slots, axis, dtype):
    n = lax.axis_size(axis)
    me = lax.axis_index(axis)
    total = take(slots, me).astype(F32)
    parts = [swap(take(slots, me ^ k), axis, k) for k in range(1, n)]
    for part in parts:
        total = total + part.astype(F32)
    return total.astype(dtype)


def by_core(mine, theirs, axis):
    c = lax.axis_index(CORE)
    first = jnp.where(c == 0, mine, theirs)
    second = jnp.where(c == 0, theirs, mine)
    return jnp.concatenate([first, second], axis=axis)


def core_cols(v):
    c = lax.axis_index(CORE)
    half = v.shape[1] // 2
    a, b = v[:, :half], v[:, half:]
    return jnp.where(c == 0, a, b), jnp.where(c == 0, b, a)


def gather_weight(w):
    mine, theirs = core_cols(w)
    got = swap(theirs, CORE, 1)
    part = by_core(mine, got, 0)
    got = everyones(part, ZZ)
    part = jnp.concatenate(pick_order(got, ZZ), axis=0)
    parts = everyones(part, HEADS)
    others = [swap(p, CORE, 1) for p in parts]
    return parts, others


def blocks_of(v):
    n = lax.axis_size(HEADS)
    size = v.shape[1] // n
    return pick_order([v[:, i * size : (i + 1) * size] for i in range(n)], HEADS)


def scatter_grad(mine, theirs):
    nh, nz = lax.axis_size(HEADS), lax.axis_size(ZZ)
    c = lax.axis_index(CORE)
    n = mine.shape[1]
    other = swap(theirs.astype(BF16), CORE, 1)
    part = (mine + other.astype(F32)).astype(BF16).reshape(nh, -1, n)
    me = lax.axis_index(HEADS)
    part = fold([take(part, me ^ k) for k in range(nh)], BF16)
    part = scatter_slots(part.reshape(nz, -1, n), ZZ, F32).reshape(2, -1, n)
    got = swap(take(part, 1 - c).astype(BF16), CORE, 1).astype(F32)
    return by_core(take(part, c), got, 1)


def all_sum(v):
    for axis in (CORE, ZZ, HEADS):
        k = 1
        while k < lax.axis_size(axis):
            other = swap(v, axis, k)
            v = v + other
            k *= 2
    return v


def pair_norm(x, first):
    sq = x * x
    low = jnp.sum(jnp.where(first, sq, 0.0), axis=-1, keepdims=True)
    high = jnp.sum(jnp.where(first, 0.0, sq), axis=-1, keepdims=True)
    return lax.rsqrt(jnp.where(first, low, high) * (1.0 / HD) + EPS)


def pair_mean(x, first):
    low = jnp.sum(jnp.where(first, x, 0.0), axis=-1, keepdims=True)
    high = jnp.sum(jnp.where(first, 0.0, x), axis=-1, keepdims=True)
    return jnp.where(first, low, high) * (1.0 / HD)


def half_turn(x, early):
    return jnp.where(early, pltpu.roll(x, PAIR - HD // 2, 1), pltpu.roll(x, HD // 2, 1))


def lane_masks(rows):
    lane = lax.broadcasted_iota(jnp.int32, (rows, PAIR), 1)
    return lane < HD, (lane % HD) < HD // 2


def rotate_kernel(qk_ref, cos_ref, sin_ref, gain_ref, q_ref, kv_ref, *, nrot, scale):
    first, early = lane_masks(qk_ref.shape[0])
    cos, sin = cos_ref[...], sin_ref[...]
    nq = q_ref.shape[1]
    cols = nq + kv_ref.shape[1]
    for p in range(cols // PAIR):
        at = slice(p * PAIR, (p + 1) * PAIR)
        x = qk_ref[:, at]
        live = min(max(nrot - 2 * p, 0), 2)
        if live:
            a = x * pair_norm(x, first) * gain_ref[:, at]
            y = a * cos + half_turn(a, early) * sin
            x = y if live == 2 else jnp.where(first, y, x)
        if p * PAIR < nq:
            q_ref[:, at] = (x * scale).astype(BF16)
        else:
            kv_ref[:, p * PAIR - nq : (p + 1) * PAIR - nq] = x.astype(BF16)


def unrotate_kernel(d_ref, x_ref, cos_ref, sin_ref, gain_ref, out_ref, dgain_ref, *, nrot, start):
    first, early = lane_masks(d_ref.shape[0])
    cos, sin = cos_ref[...], sin_ref[...]
    total = jnp.zeros((1, PAIR), F32)
    for p in range(d_ref.shape[1] // PAIR):
        at = slice(p * PAIR, (p + 1) * PAIR)
        d = d_ref[:, at]
        live = min(max(nrot - 2 * p, 0), 2)
        if live:
            there = slice(start + p * PAIR, start + (p + 1) * PAIR)
            x = x_ref[:, there]
            scale = pair_norm(x, first)
            unit = x * scale
            da = d * cos + half_turn(d * sin, early)
            if live == 1:
                da = jnp.where(first, da, 0.0)
            total = total + jnp.sum(da * unit, axis=0, keepdims=True)
            n = da * gain_ref[:, there]
            y = scale * (n - unit * pair_mean(n * unit, first))
            d = y if live == 2 else jnp.where(first, y, d)
        out_ref[:, at] = d.astype(BF16)
    dgain_ref[...] = total


def dot_nt(a, b):
    return lax.dot_general(a, b, (((1,), (1,)), ((), ())), preferred_element_type=F32)


def dot_tn(a, b):
    return lax.dot_general(a, b, (((0,), (0,)), ((), ())), preferred_element_type=F32)


def head_rows(ref, rows, g, per):
    return jnp.concatenate(
        [ref[rows, (g * per + i) * HD : (g * per + i + 1) * HD] for i in range(per)], axis=0
    )


def head_lanes(v, per):
    size = v.shape[0] // per
    return jnp.concatenate([v[i * size : (i + 1) * size] for i in range(per)], axis=1)


def attend_kernel(q_ref, kv_ref, segq_ref, segk_ref, out_ref, *, kvh, per, block):
    rows, keys = q_ref.shape[0], kv_ref.shape[0]
    band = keys - rows + block
    for lo in range(0, rows, block):
        at, near = slice(lo, lo + block), slice(lo, lo + band)
        place_q = lax.broadcasted_iota(jnp.int32, (block, band), 0) + (keys - rows)
        place_k = lax.broadcasted_iota(jnp.int32, (block, band), 1)
        bias = jnp.where(
            (segq_ref[at, :] == segk_ref[:, near]) & (place_q >= place_k), 0.0, NEG
        )
        for g in range(kvh):
            k = kv_ref[near, g * HD : (g + 1) * HD]
            v = kv_ref[near, (kvh + g) * HD : (kvh + g + 1) * HD]
            s = dot_nt(head_rows(q_ref, at, g, per), k)
            s = s.reshape(per, block, band) + bias[None]
            e = jnp.exp(s - jnp.max(s, axis=-1, keepdims=True))
            p = e * (1.0 / jnp.sum(e, axis=-1, keepdims=True))
            o = jnp.dot(
                p.astype(BF16).reshape(per * block, band), v, preferred_element_type=F32
            )
            out_ref[at, g * per * HD : (g + 1) * per * HD] = head_lanes(o, per).astype(BF16)


def attend_back_kernel(
    q_ref, kv_ref, d_ref, segq_ref, segk_ref, dq_ref, dkv_ref, *, kvh, per, block, scale
):
    rows, keys = q_ref.shape[0], kv_ref.shape[0]
    band = keys - rows + block
    dkv_ref[...] = jnp.zeros_like(dkv_ref)
    for lo in range(0, rows, block):
        at, near = slice(lo, lo + block), slice(lo, lo + band)
        place_k = lax.broadcasted_iota(jnp.int32, (band, block), 0)
        place_q = lax.broadcasted_iota(jnp.int32, (band, block), 1) + (keys - rows)
        bias = jnp.where(
            (segk_ref[near, :] == segq_ref[:, at]) & (place_q >= place_k), 0.0, NEG
        )
        bias = jnp.concatenate([bias] * per, axis=1)
        for g in range(kvh):
            ks = slice(g * HD, (g + 1) * HD)
            vs = slice((kvh + g) * HD, (kvh + g + 1) * HD)
            k, v = kv_ref[near, ks], kv_ref[near, vs]
            q, d = head_rows(q_ref, at, g, per), head_rows(d_ref, at, g, per)
            s = dot_nt(k, q) + bias
            e = jnp.exp(s - jnp.max(s, axis=0, keepdims=True))
            p = e * (1.0 / jnp.sum(e, axis=0, keepdims=True))
            dp = dot_nt(v, d)
            delta = jnp.sum(p * dp, axis=0, keepdims=True)
            ds = (p * (dp - delta)).astype(BF16)
            dkv_ref[near, ks] += jnp.dot(ds, q, preferred_element_type=F32)
            dkv_ref[near, vs] += jnp.dot(p.astype(BF16), d, preferred_element_type=F32)
            dq = dot_tn(ds, k) * scale
            dq_ref[at, g * per * HD : (g + 1) * per * HD] = head_lanes(dq, per)


def weight_grad_kernel(*refs, chunks, parts):
    lefts, rights, out_ref = refs[:chunks], refs[chunks:-1], refs[-1]
    size = rights[0].shape[1]
    for i in range(parts):
        total = sum(
            dot_tn(left[...], rights[k * parts + i][...]) for k, left in enumerate(lefts)
        )
        out_ref[:, i * size : (i + 1) * size] = total.astype(BF16)


def in_hbm(v):
    return pltpu.with_memory_space_constraint(v, pltpu.HBM)


def weight_grad(lefts, rights):
    chunks, parts = len(lefts), len(rights[0])
    rows, width = lefts[0].shape
    size = rights[0][0].shape[1]
    block = min(width, 256)
    right_spec = pl.BlockSpec((rows, size), lambda i: (0, 0))
    return pl.pallas_call(
        functools.partial(weight_grad_kernel, chunks=chunks, parts=parts),
        grid=(width // block,),
        in_specs=[pl.BlockSpec((rows, block), lambda i: (0, i))] * chunks
        + [right_spec] * (chunks * parts),
        out_specs=pl.BlockSpec((block, parts * size), lambda i: (i, 0)),
        out_shape=pltpu.HBM((width, parts * size), BF16),
        compiler_params=pltpu.CompilerParams(vmem_limit_bytes=20 << 20),
    )(*[in_hbm(a) for a in [*lefts, *[r for row in rights for r in row]]])


def local_call(kernel, outs, *args):
    return pl.pallas_call(
        kernel,
        out_shape=[jax.ShapeDtypeStruct(shape, dtype) for shape, dtype in outs],
        compiler_params=pltpu.CompilerParams(vmem_limit_bytes=16 << 20),
    )(*args)


def shards(
    hidden_in,
    segment_ids,
    attn_gain,
    w_query,
    w_key,
    w_value,
    query_gain,
    key_gain,
    w_out,
    ffn_gain,
    w_gate,
    w_up,
    w_down,
    cotangent,
):
    groups, local_len, width = hidden_in.shape
    seq_len = segment_ids.shape[1]
    nh = lax.axis_size(HEADS)
    h = lax.axis_index(HEADS)
    nq, nkv = w_query.shape[1], w_key.shape[1]
    q_heads, kv_heads = nq // HD, nkv // HD
    per_kv = q_heads // kv_heads
    ff = w_gate.shape[1] // nh
    shard = w_gate.shape[0]
    scale = HD ** (-0.5)
    longest = seq_len // 4
    nhalo = min(-(-(longest - 1) // local_len), nh - 1)

    def columns_of(at):
        return jnp.concatenate(
            [lax.dynamic_slice_in_dim(w, at * ff, ff, 1) for w in (w_gate, w_up, w_down)], axis=1
        )

    got = [swap(columns_of(h ^ k), HEADS, k) for k in range(1, nh)]
    buf = jnp.stack(pick_order([columns_of(h)] + got, HEADS))
    npad = -(nq + 2 * nkv) % 256
    spare = jnp.zeros((shard, npad), BF16)
    qkv_parts, qkv_others = gather_weight(
        jnp.concatenate([w_query, w_key, w_value, spare], axis=1)
    )
    o_parts, o_others = gather_weight(w_out)
    w_all = lax.all_gather(buf, ROWS, axis=1, tiled=True).reshape(width, -1)
    w_gu, w_dn = w_all[:, : 2 * ff], w_all[:, 2 * ff :]

    grad_y = cotangent.reshape(-1, width)
    g_chunks = everyones(grad_y, HEADS)

    seg = segment_ids.reshape(-1)
    mine = lax.dynamic_slice_in_dim(positions_of(seg), h * local_len, local_len, 0)
    cos, sin = rotary_tables(mine)

    x = hidden_in.astype(F32).reshape(-1, width)
    inv_one = norm_scale(x)
    unit_one = x * inv_one
    normed = (unit_one * attn_gain).astype(BF16)
    blocks = blocks_of(normed)
    qkv_mine = sum(mm(b, w) for b, w in zip(blocks, qkv_parts))
    qkv_theirs = sum(mm(b, w) for b, w in zip(blocks, qkv_others))
    qkv = by_core(qkv_mine, qkv_theirs, 1)
    gains = jnp.concatenate(
        [
            jnp.tile(query_gain, q_heads),
            jnp.tile(key_gain, kv_heads),
            jnp.zeros((nkv,), F32),
        ]
    )[None]
    q_rot, kv = local_call(
        functools.partial(rotate_kernel, nrot=q_heads + kv_heads, scale=scale),
        [((local_len, nq), BF16), ((local_len, 2 * nkv), BF16)],
        qkv,
        cos,
        sin,
        gains,
    )
    pieces = [
        lax.ppermute(kv, HEADS, [(i, i + s) for i in range(nh - s)])
        for s in range(nhalo, 0, -1)
    ] + [kv]
    kv_ext = jnp.concatenate(pieces, axis=0)
    nkeys = kv_ext.shape[0]
    seg_pad = jnp.concatenate([jnp.full((nhalo * local_len,), -1, jnp.int32), seg])
    seg_k = lax.dynamic_slice_in_dim(seg_pad, h * local_len, nkeys, 0)
    seg_q = lax.dynamic_slice_in_dim(seg, h * local_len, local_len, 0)
    shape = dict(kvh=kv_heads, per=per_kv, block=min(local_len, 128))
    (mixed,) = local_call(
        functools.partial(attend_kernel, **shape),
        [((local_len, nq), BF16)],
        q_rot,
        kv_ext,
        seg_q[:, None],
        seg_k[None],
    )
    mixed_mine, mixed_theirs = core_cols(mixed)
    attn = [
        dot_nt(mixed_mine, p) + dot_nt(mixed_theirs, q) for p, q in zip(o_parts, o_others)
    ]
    attn = jnp.concatenate(pick_order(attn, HEADS), axis=1)
    resid = x + attn
    inv_two = norm_scale(resid)
    unit_two = resid * inv_two
    normed_two = (unit_two * ffn_gain).astype(BF16)

    o_part, o_other = settle(o_parts, HEADS), settle(o_others, HEADS)
    qkv_part, qkv_other = settle(qkv_parts, HEADS), settle(qkv_others, HEADS)
    n_chunks = everyones(normed_two, HEADS)
    outs, backs, d_all = [], [], []
    for k in range(nh):
        gu = mm(n_chunks[k], w_gu)
        gate, up = gu[:, :ff], gu[:, ff:]
        sig = jax.nn.sigmoid(gate)
        act = gate * sig
        hidden = (act * up).astype(BF16)
        d_hidden = mm(g_chunks[k], w_dn)
        d_gate = (d_hidden * up * sig * (1.0 + gate * (1.0 - sig))).astype(BF16)
        d_up = (d_hidden * act).astype(BF16)
        d_gu = jnp.concatenate([d_gate, d_up], axis=1)
        back = dot_nt(d_gu, w_gu)
        if k:
            back = swap(back.astype(BF16), HEADS, k)
            back = back.astype(F32)
        out = dot_nt(hidden, w_dn)
        outs.append(out.astype(BF16) if k else out)
        backs.append(back)
        d_all.append(([d_gate, d_up], [hidden]))
    layer_out = (resid + fold(outs, F32)).astype(BF16).reshape(groups, local_len, width)

    def column_grads(grad, count):
        slots = lax.psum_scatter(
            grad.reshape(nh, -1, count * ff), ROWS, scatter_dimension=1, tiled=True
        )
        got = [swap(take(slots, h ^ k), HEADS, k) for k in range(1, nh)]
        full = pick_order([take(slots, h)] + got, HEADS)
        return [
            jnp.concatenate([p[:, i * ff : (i + 1) * ff] for p in full], axis=1).astype(F32)
            for i in range(count)
        ]

    grad_dn = weight_grad(g_chunks, [d[1] for d in d_all])
    grad_gu = weight_grad(n_chunks, [d[0] for d in d_all])
    (r_down,) = column_grads(grad_dn, 1)
    r_gate, r_up = column_grads(grad_gu, 2)

    d_normed_two = sum(backs)
    g_ffn = jnp.sum(d_normed_two * unit_two, axis=0)
    d_resid = grad_y.astype(F32) + norm_back(d_normed_two, unit_two, inv_two, ffn_gain)
    d_attn = d_resid.astype(BF16)
    go_theirs = dot_tn(d_attn, mixed_theirs)
    go_mine = dot_tn(d_attn, mixed_mine)
    r_out = scatter_grad(go_mine, go_theirs)
    d_mixed_mine = mm(d_attn, o_part).astype(BF16)
    d_mixed_theirs = mm(d_attn, o_other).astype(BF16)
    d_mixed = by_core(d_mixed_mine, d_mixed_theirs, 1)

    d_q, d_kv = local_call(
        functools.partial(attend_back_kernel, scale=scale, **shape),
        [((local_len, nq), F32), ((nkeys, 2 * nkv), F32)],
        q_rot,
        kv_ext,
        d_mixed,
        seg_q[None],
        seg_k[:, None],
    )
    d_kv_loc = d_kv[nhalo * local_len :]
    for s in range(1, nhalo + 1):
        lo = (nhalo - s) * local_len
        piece = d_kv[lo : lo + local_len].astype(BF16)
        piece = lax.ppermute(piece, HEADS, [(i + s, i) for i in range(nh - s)])
        d_kv_loc = d_kv_loc + piece.astype(F32)

    def unrotate(d, nrot, start):
        return local_call(
            functools.partial(unrotate_kernel, nrot=nrot, start=start),
            [(d.shape, BF16), ((1, PAIR), F32)],
            d,
            qkv,
            cos,
            sin,
            gains,
        )

    d_q_raw, g_qgain = unrotate(d_q, q_heads, 0)
    d_kv_raw, g_kgain = unrotate(d_kv_loc, kv_heads, nq)
    g_qgain = g_qgain[0, :HD] + g_qgain[0, HD:]
    g_kgain = g_kgain[0, :HD] + g_kgain[0, HD:]
    spare = jnp.zeros((local_len, npad), BF16)
    d_mine, d_theirs = core_cols(jnp.concatenate([d_q_raw, d_kv_raw, spare], axis=1))
    gq_theirs = dot_tn(normed, d_theirs)
    gq_mine = dot_tn(normed, d_mine)
    r_qkv = scatter_grad(gq_mine, gq_theirs)
    d_normed = dot_nt(d_mine, qkv_part)
    d_normed = d_normed + dot_nt(d_theirs, qkv_other)
    g_attn = jnp.sum(d_normed * unit_one, axis=0)
    grad_in = (
        (d_resid + norm_back(d_normed, unit_one, inv_one, attn_gain))
        .astype(BF16)
        .reshape(groups, local_len, width)
    )
    small = all_sum(jnp.concatenate([g_attn, g_ffn, g_qgain, g_kgain]))
    nz = lax.axis_size(ZZ)
    at = ((h * nz + lax.axis_index(ZZ)) * 2 + lax.axis_index(CORE)) * shard
    r_attn = lax.dynamic_slice_in_dim(small, at, shard, 0)
    r_ffn = lax.dynamic_slice_in_dim(small, width + at, shard, 0)
    return (
        layer_out,
        grad_in,
        r_attn,
        r_qkv[:, :nq],
        r_qkv[:, nq : nq + nkv],
        r_qkv[:, nq + nkv : nq + 2 * nkv],
        small[2 * width : 2 * width + HD],
        small[2 * width + HD :],
        r_out,
        r_ffn,
        r_gate,
        r_up,
        r_down,
    )


def solution(mesh):
    nh, nr = mesh.shape[HEADS], mesh.shape["rows"]
    fine = Mesh(mesh.devices.reshape(nh, nr // 2, 2), ALL)
    tokens = P(ROWS, HEADS, None)
    weight = P(ALL, None)
    vector = P(ALL)
    in_specs = (
        tokens,
        P(ROWS, None),
        P(),
        weight,
        weight,
        weight,
        P(),
        P(),
        weight,
        P(),
        weight,
        weight,
        weight,
        tokens,
    )
    out_specs = (
        tokens,
        tokens,
        vector,
        weight,
        weight,
        weight,
        P(),
        P(),
        weight,
        vector,
        weight,
        weight,
        weight,
    )

    return jax.shard_map(
        shards, mesh=fine, in_specs=in_specs, out_specs=out_specs, check_vma=False
    )
```

```python
import functools
import math

import jax
import jax.numpy as jnp
from jax import lax
from jax.experimental import pallas as pl
from jax.experimental.pallas import tpu as pltpu
from jax.sharding import Mesh
from jax.sharding import PartitionSpec as P


HEADS, ZZ, CORE = "heads", "zz", "core"

HD = 64
PAIR = 2 * HD
EPS = 1e-06
NEG = -1e30
THETA = 10000.0
ROWS = (ZZ, CORE)
ALL = (HEADS, ZZ, CORE)
F32 = jnp.float32
BF16 = jnp.bfloat16


def norm_scale(v):
    return lax.rsqrt(jnp.mean(v * v, axis=-1, keepdims=True) + EPS)


def norm_back(grad_n, unit_v, scale, gain):
    scaled = grad_n * gain
    return scale * (scaled - unit_v * jnp.mean(scaled * unit_v, axis=-1, keepdims=True))


def positions_of(segment_ids):
    places = lax.broadcasted_iota(jnp.int32, segment_ids.shape, 0)
    first = jnp.concatenate(
        [jnp.ones_like(segment_ids[:1]), (segment_ids[1:] != segment_ids[:-1]).astype(jnp.int32)]
    )
    return places - lax.cummax(places * first, axis=0)


def rotary_tables(positions):
    half = HD // 2
    freqs = jnp.exp(jnp.arange(half, dtype=F32) * (-2.0 * math.log(THETA) / HD))
    angles = positions.astype(F32)[:, None] * freqs
    angles = jnp.concatenate([angles, angles], axis=-1)
    sign = jnp.where(jnp.arange(HD) < half, -1.0, 1.0)
    return jnp.tile(jnp.cos(angles), (1, 2)), jnp.tile(jnp.sin(angles) * sign, (1, 2))


def mm(a, b):
    return jnp.dot(a, b, preferred_element_type=F32)


def swap(v, axis, k):
    n = lax.axis_size(axis)
    return lax.ppermute(v, axis, [(i, i ^ k) for i in range(n)])


def put(buf, v, i):
    return lax.dynamic_update_index_in_dim(buf, v, i, 0)


def take(buf, i):
    return lax.dynamic_index_in_dim(buf, i, 0, keepdims=False)


def everyones(v, axis):
    n = lax.axis_size(axis)
    if axis != HEADS or n != 4:
        return [v] + [swap(v, axis, k) for k in range(1, n)]
    half = v.shape[0] // 2
    one, two = swap(v, axis, 1), swap(v, axis, 2)
    low = swap(one[:half], axis, 2)
    high = swap(two[half:], axis, 1)
    return [v, one, two, jnp.concatenate([low, high], axis=0)]


def everyones_early(v):
    if lax.axis_size(HEADS) != 4:
        return everyones(v, HEADS)
    half = v.shape[0] // 2
    low, high = v[:half], v[half:]
    low_one, low_two = swap(low, HEADS, 1), swap(low, HEADS, 2)
    high_one, high_two = swap(high, HEADS, 1), swap(high, HEADS, 2)
    low_far = swap(low_one, HEADS, 2)
    high_far = swap(high_two, HEADS, 1)
    pairs = ((low_one, high_one), (low_two, high_two), (low_far, high_far))
    return [v] + [jnp.concatenate(p, axis=0) for p in pairs]


def settle(got, axis):
    me = lax.axis_index(axis)
    buf = jnp.zeros((len(got), *got[0].shape), got[0].dtype)
    for k, piece in enumerate(got):
        buf = put(buf, piece, me ^ k)
    return buf.reshape(-1, got[0].shape[-1])


def fold(parts, dtype):
    n = len(parts)
    if n != 4:
        got = [swap(p.astype(BF16), HEADS, k) for k, p in enumerate(parts) if k]
        return sum((g.astype(F32) for g in got), parts[0].astype(F32)).astype(dtype)
    half = parts[0].shape[0] // 2
    low, high = [p[:half] for p in parts], [p[half:] for p in parts]
    one = jnp.stack([low[1], low[3]]).astype(BF16)
    two = jnp.stack([high[2], high[3]]).astype(BF16)
    one, two = swap(one, HEADS, 1), swap(two, HEADS, 2)
    low_on = (low[2].astype(F32) + one[1].astype(F32)).astype(BF16)
    high_on = (high[1].astype(F32) + two[1].astype(F32)).astype(BF16)
    low_end = swap(low_on, HEADS, 2)
    high_end = swap(high_on, HEADS, 1)
    low_sum = low[0].astype(F32) + one[0].astype(F32) + low_end.astype(F32)
    high_sum = high[0].astype(F32) + two[0].astype(F32) + high_end.astype(F32)
    return jnp.concatenate([low_sum, high_sum], axis=0).astype(dtype)


def pick_order(got, axis):
    me = lax.axis_index(axis)
    n = len(got)
    out = []
    for j in range(n):
        piece = got[j]
        for i in range(1, n):
            piece = jnp.where(me == i, got[j ^ i], piece)
        out.append(piece)
    return out


def scatter_slots(slots, axis, dtype):
    n = lax.axis_size(axis)
    me = lax.axis_index(axis)
    total = take(slots, me).astype(F32)
    parts = [swap(take(slots, me ^ k), axis, k) for k in range(1, n)]
    for part in parts:
        total = total + part.astype(F32)
    return total.astype(dtype)


def by_core(mine, theirs, axis):
    c = lax.axis_index(CORE)
    first = jnp.where(c == 0, mine, theirs)
    second = jnp.where(c == 0, theirs, mine)
    return jnp.concatenate([first, second], axis=axis)


def core_cols(v):
    c = lax.axis_index(CORE)
    half = v.shape[1] // 2
    a, b = v[:, :half], v[:, half:]
    return jnp.where(c == 0, a, b), jnp.where(c == 0, b, a)


def gather_weight(w):
    mine, theirs = core_cols(w)
    got = swap(theirs, CORE, 1)
    part = by_core(mine, got, 0)
    got = everyones(part, ZZ)
    part = jnp.concatenate(pick_order(got, ZZ), axis=0)
    parts = everyones(part, HEADS)
    others = [swap(p, CORE, 1) for p in parts]
    return parts, others


def blocks_of(v):
    n = lax.axis_size(HEADS)
    size = v.shape[1] // n
    return pick_order([v[:, i * size : (i + 1) * size] for i in range(n)], HEADS)


def scatter_grad(mine, theirs):
    nh, nz = lax.axis_size(HEADS), lax.axis_size(ZZ)
    c = lax.axis_index(CORE)
    n = mine.shape[1]
    other = swap(theirs.astype(BF16), CORE, 1)
    part = (mine + other.astype(F32)).astype(BF16).reshape(nh, -1, n)
    me = lax.axis_index(HEADS)
    part = fold([take(part, me ^ k) for k in range(nh)], BF16)
    part = scatter_slots(part.reshape(nz, -1, n), ZZ, F32).reshape(2, -1, n)
    got = swap(take(part, 1 - c).astype(BF16), CORE, 1).astype(F32)
    return by_core(take(part, c), got, 1)


def all_sum(v):
    for axis in (CORE, ZZ, HEADS):
        k = 1
        while k < lax.axis_size(axis):
            other = swap(v, axis, k)
            v = v + other
            k *= 2
    return v


def pair_norm(x, first):
    sq = x * x
    low = jnp.sum(jnp.where(first, sq, 0.0), axis=-1, keepdims=True)
    high = jnp.sum(jnp.where(first, 0.0, sq), axis=-1, keepdims=True)
    return lax.rsqrt(jnp.where(first, low, high) * (1.0 / HD) + EPS)


def pair_mean(x, first):
    low = jnp.sum(jnp.where(first, x, 0.0), axis=-1, keepdims=True)
    high = jnp.sum(jnp.where(first, 0.0, x), axis=-1, keepdims=True)
    return jnp.where(first, low, high) * (1.0 / HD)


def half_turn(x, early):
    return jnp.where(early, pltpu.roll(x, PAIR - HD // 2, 1), pltpu.roll(x, HD // 2, 1))


def lane_masks(rows):
    lane = lax.broadcasted_iota(jnp.int32, (rows, PAIR), 1)
    return lane < HD, (lane % HD) < HD // 2


def rotate_kernel(qk_ref, cos_ref, sin_ref, gain_ref, q_ref, kv_ref, *, nrot, scale):
    first, early = lane_masks(qk_ref.shape[0])
    cos, sin = cos_ref[...], sin_ref[...]
    nq = q_ref.shape[1]
    cols = nq + kv_ref.shape[1]
    for p in range(cols // PAIR):
        at = slice(p * PAIR, (p + 1) * PAIR)
        x = qk_ref[:, at]
        live = min(max(nrot - 2 * p, 0), 2)
        if live:
            a = x * pair_norm(x, first) * gain_ref[:, at]
            y = a * cos + half_turn(a, early) * sin
            x = y if live == 2 else jnp.where(first, y, x)
        if p * PAIR < nq:
            q_ref[:, at] = (x * scale).astype(BF16)
        else:
            kv_ref[:, p * PAIR - nq : (p + 1) * PAIR - nq] = x.astype(BF16)


def unrotate_kernel(d_ref, x_ref, cos_ref, sin_ref, gain_ref, out_ref, dgain_ref, *, nrot, start):
    first, early = lane_masks(d_ref.shape[0])
    cos, sin = cos_ref[...], sin_ref[...]
    total = jnp.zeros((1, PAIR), F32)
    for p in range(d_ref.shape[1] // PAIR):
        at = slice(p * PAIR, (p + 1) * PAIR)
        d = d_ref[:, at]
        live = min(max(nrot - 2 * p, 0), 2)
        if live:
            there = slice(start + p * PAIR, start + (p + 1) * PAIR)
            x = x_ref[:, there]
            scale = pair_norm(x, first)
            unit = x * scale
            da = d * cos + half_turn(d * sin, early)
            if live == 1:
                da = jnp.where(first, da, 0.0)
            total = total + jnp.sum(da * unit, axis=0, keepdims=True)
            n = da * gain_ref[:, there]
            y = scale * (n - unit * pair_mean(n * unit, first))
            d = y if live == 2 else jnp.where(first, y, d)
        out_ref[:, at] = d.astype(BF16)
    dgain_ref[...] = total


def dot_nt(a, b):
    return lax.dot_general(a, b, (((1,), (1,)), ((), ())), preferred_element_type=F32)


def dot_tn(a, b):
    return lax.dot_general(a, b, (((0,), (0,)), ((), ())), preferred_element_type=F32)


def head_rows(ref, rows, g, per):
    return jnp.concatenate(
        [ref[rows, (g * per + i) * HD : (g * per + i + 1) * HD] for i in range(per)], axis=0
    )


def head_lanes(v, per):
    size = v.shape[0] // per
    return jnp.concatenate([v[i * size : (i + 1) * size] for i in range(per)], axis=1)


def attend_kernel(q_ref, kv_ref, segq_ref, segk_ref, out_ref, *, kvh, per, block):
    rows, keys = q_ref.shape[0], kv_ref.shape[0]
    band = keys - rows + block
    for lo in range(0, rows, block):
        at, near = slice(lo, lo + block), slice(lo, lo + band)
        place_q = lax.broadcasted_iota(jnp.int32, (block, band), 0) + (keys - rows)
        place_k = lax.broadcasted_iota(jnp.int32, (block, band), 1)
        bias = jnp.where(
            (segq_ref[at, :] == segk_ref[:, near]) & (place_q >= place_k), 0.0, NEG
        )
        for g in range(kvh):
            k = kv_ref[near, g * HD : (g + 1) * HD]
            v = kv_ref[near, (kvh + g) * HD : (kvh + g + 1) * HD]
            s = dot_nt(head_rows(q_ref, at, g, per), k)
            s = s.reshape(per, block, band) + bias[None]
            e = jnp.exp(s - jnp.max(s, axis=-1, keepdims=True))
            p = e * (1.0 / jnp.sum(e, axis=-1, keepdims=True))
            o = jnp.dot(
                p.astype(BF16).reshape(per * block, band), v, preferred_element_type=F32
            )
            out_ref[at, g * per * HD : (g + 1) * per * HD] = head_lanes(o, per).astype(BF16)


def attend_back_kernel(
    q_ref, kv_ref, d_ref, segq_ref, segk_ref, dq_ref, dkv_ref, *, kvh, per, block, scale
):
    rows, keys = q_ref.shape[0], kv_ref.shape[0]
    band = keys - rows + block
    dkv_ref[...] = jnp.zeros_like(dkv_ref)
    for lo in range(0, rows, block):
        at, near = slice(lo, lo + block), slice(lo, lo + band)
        place_k = lax.broadcasted_iota(jnp.int32, (band, block), 0)
        place_q = lax.broadcasted_iota(jnp.int32, (band, block), 1) + (keys - rows)
        bias = jnp.where(
            (segk_ref[near, :] == segq_ref[:, at]) & (place_q >= place_k), 0.0, NEG
        )
        bias = jnp.concatenate([bias] * per, axis=1)
        for g in range(kvh):
            ks = slice(g * HD, (g + 1) * HD)
            vs = slice((kvh + g) * HD, (kvh + g + 1) * HD)
            k, v = kv_ref[near, ks], kv_ref[near, vs]
            q, d = head_rows(q_ref, at, g, per), head_rows(d_ref, at, g, per)
            s = dot_nt(k, q) + bias
            e = jnp.exp(s - jnp.max(s, axis=0, keepdims=True))
            p = e * (1.0 / jnp.sum(e, axis=0, keepdims=True))
            dp = dot_nt(v, d)
            delta = jnp.sum(p * dp, axis=0, keepdims=True)
            ds = (p * (dp - delta)).astype(BF16)
            dkv_ref[near, ks] += jnp.dot(ds, q, preferred_element_type=F32)
            dkv_ref[near, vs] += jnp.dot(p.astype(BF16), d, preferred_element_type=F32)
            dq = dot_tn(ds, k) * scale
            dq_ref[at, g * per * HD : (g + 1) * per * HD] = head_lanes(dq, per)


def weight_grad_kernel(*refs, chunks, parts):
    lefts, rights, out_ref = refs[:chunks], refs[chunks:-1], refs[-1]
    size = rights[0].shape[1]
    for i in range(parts):
        total = sum(
            dot_tn(left[...], rights[k * parts + i][...]) for k, left in enumerate(lefts)
        )
        out_ref[:, i * size : (i + 1) * size] = total.astype(BF16)


def in_hbm(v):
    return pltpu.with_memory_space_constraint(v, pltpu.HBM)


def weight_grad(lefts, rights):
    chunks, parts = len(lefts), len(rights[0])
    rows, width = lefts[0].shape
    size = rights[0][0].shape[1]
    block = min(width, 256)
    right_spec = pl.BlockSpec((rows, size), lambda i: (0, 0))
    return pl.pallas_call(
        functools.partial(weight_grad_kernel, chunks=chunks, parts=parts),
        grid=(width // block,),
        in_specs=[pl.BlockSpec((rows, block), lambda i: (0, i))] * chunks
        + [right_spec] * (chunks * parts),
        out_specs=pl.BlockSpec((block, parts * size), lambda i: (i, 0)),
        out_shape=pltpu.HBM((width, parts * size), BF16),
        compiler_params=pltpu.CompilerParams(vmem_limit_bytes=20 << 20),
    )(*[in_hbm(a) for a in [*lefts, *[r for row in rights for r in row]]])


def local_call(kernel, outs, *args):
    return pl.pallas_call(
        kernel,
        out_shape=[jax.ShapeDtypeStruct(shape, dtype) for shape, dtype in outs],
        compiler_params=pltpu.CompilerParams(vmem_limit_bytes=16 << 20),
    )(*args)


def shards(
    hidden_in,
    segment_ids,
    attn_gain,
    w_query,
    w_key,
    w_value,
    query_gain,
    key_gain,
    w_out,
    ffn_gain,
    w_gate,
    w_up,
    w_down,
    cotangent,
):
    groups, local_len, width = hidden_in.shape
    seq_len = segment_ids.shape[1]
    nh = lax.axis_size(HEADS)
    h = lax.axis_index(HEADS)
    nq, nkv = w_query.shape[1], w_key.shape[1]
    q_heads, kv_heads = nq // HD, nkv // HD
    per_kv = q_heads // kv_heads
    ff = w_gate.shape[1] // nh
    shard = w_gate.shape[0]
    scale = HD ** (-0.5)
    longest = seq_len // 4
    nhalo = min(-(-(longest - 1) // local_len), nh - 1)

    def columns_of(at):
        return jnp.concatenate(
            [lax.dynamic_slice_in_dim(w, at * ff, ff, 1) for w in (w_gate, w_up, w_down)], axis=1
        )

    got = [swap(columns_of(h ^ k), HEADS, k) for k in range(1, nh)]
    buf = jnp.stack(pick_order([columns_of(h)] + got, HEADS))
    npad = -(nq + 2 * nkv) % 256
    spare = jnp.zeros((shard, npad), BF16)
    qkv_parts, qkv_others = gather_weight(
        jnp.concatenate([w_query, w_key, w_value, spare], axis=1)
    )
    o_parts, o_others = gather_weight(w_out)
    w_all = lax.all_gather(buf, ROWS, axis=1, tiled=True).reshape(width, -1)
    w_gu, w_dn = w_all[:, : 2 * ff], w_all[:, 2 * ff :]

    grad_y = cotangent.reshape(-1, width)
    g_chunks = everyones_early(grad_y)

    seg = segment_ids.reshape(-1)
    mine = lax.dynamic_slice_in_dim(positions_of(seg), h * local_len, local_len, 0)
    cos, sin = rotary_tables(mine)

    x = hidden_in.astype(F32).reshape(-1, width)
    inv_one = norm_scale(x)
    unit_one = x * inv_one
    normed = (unit_one * attn_gain).astype(BF16)
    blocks = blocks_of(normed)
    qkv_mine = sum(mm(b, w) for b, w in zip(blocks, qkv_parts))
    qkv_theirs = sum(mm(b, w) for b, w in zip(blocks, qkv_others))
    qkv = by_core(qkv_mine, qkv_theirs, 1)
    gains = jnp.concatenate(
        [
            jnp.tile(query_gain, q_heads),
            jnp.tile(key_gain, kv_heads),
            jnp.zeros((nkv,), F32),
        ]
    )[None]
    q_rot, kv = local_call(
        functools.partial(rotate_kernel, nrot=q_heads + kv_heads, scale=scale),
        [((local_len, nq), BF16), ((local_len, 2 * nkv), BF16)],
        qkv,
        cos,
        sin,
        gains,
    )
    pieces = [
        lax.ppermute(kv, HEADS, [(i, i + s) for i in range(nh - s)])
        for s in range(nhalo, 0, -1)
    ] + [kv]
    kv_ext = jnp.concatenate(pieces, axis=0)
    nkeys = kv_ext.shape[0]
    seg_pad = jnp.concatenate([jnp.full((nhalo * local_len,), -1, jnp.int32), seg])
    seg_k = lax.dynamic_slice_in_dim(seg_pad, h * local_len, nkeys, 0)
    seg_q = lax.dynamic_slice_in_dim(seg, h * local_len, local_len, 0)
    shape = dict(kvh=kv_heads, per=per_kv, block=min(local_len, 128))
    (mixed,) = local_call(
        functools.partial(attend_kernel, **shape),
        [((local_len, nq), BF16)],
        q_rot,
        kv_ext,
        seg_q[:, None],
        seg_k[None],
    )
    mixed_mine, mixed_theirs = core_cols(mixed)
    attn = [
        dot_nt(mixed_mine, p) + dot_nt(mixed_theirs, q) for p, q in zip(o_parts, o_others)
    ]
    attn = jnp.concatenate(pick_order(attn, HEADS), axis=1)
    resid = x + attn
    inv_two = norm_scale(resid)
    unit_two = resid * inv_two
    normed_two = (unit_two * ffn_gain).astype(BF16)

    qkv_part, qkv_other = settle(qkv_parts, HEADS), settle(qkv_others, HEADS)
    n_chunks = everyones(normed_two, HEADS)
    outs, backs, d_all = [], [], []
    for k in range(nh):
        gu = mm(n_chunks[k], w_gu)
        gate, up = gu[:, :ff], gu[:, ff:]
        sig = jax.nn.sigmoid(gate)
        act = gate * sig
        hidden = (act * up).astype(BF16)
        d_hidden = mm(g_chunks[k], w_dn)
        d_gate = (d_hidden * up * sig * (1.0 + gate * (1.0 - sig))).astype(BF16)
        d_up = (d_hidden * act).astype(BF16)
        d_gu = jnp.concatenate([d_gate, d_up], axis=1)
        back = dot_nt(d_gu, w_gu)
        if not k:
            back = lax.optimization_barrier(back)
        if k:
            back = swap(back.astype(BF16), HEADS, k)
            back = back.astype(F32)
        out = dot_nt(hidden, w_dn)
        outs.append(out.astype(BF16) if k else out)
        backs.append(back)
        d_all.append(([d_gate, d_up], [hidden]))
    layer_out = (resid + fold(outs, F32)).astype(BF16).reshape(groups, local_len, width)

    def column_grads(grad, count):
        slots = lax.psum_scatter(
            grad.reshape(nh, -1, count * ff), ROWS, scatter_dimension=1, tiled=True
        )
        got = [swap(take(slots, h ^ k), HEADS, k) for k in range(1, nh)]
        full = pick_order([take(slots, h)] + got, HEADS)
        return [
            jnp.concatenate([p[:, i * ff : (i + 1) * ff] for p in full], axis=1).astype(F32)
            for i in range(count)
        ]

    grad_dn = weight_grad(g_chunks, [d[1] for d in d_all])
    grad_gu = weight_grad(n_chunks, [d[0] for d in d_all])
    (r_down,) = column_grads(grad_dn, 1)
    r_gate, r_up = column_grads(grad_gu, 2)

    d_normed_two = sum(backs)
    g_ffn = jnp.sum(d_normed_two * unit_two, axis=0)
    d_resid = grad_y.astype(F32) + norm_back(d_normed_two, unit_two, inv_two, ffn_gain)
    d_attn = d_resid.astype(BF16)
    go_theirs = dot_tn(d_attn, mixed_theirs)
    go_mine = dot_tn(d_attn, mixed_mine)
    r_out = scatter_grad(go_mine, go_theirs)
    d_blocks = blocks_of(d_attn)
    d_mixed_mine = sum(mm(b, w) for b, w in zip(d_blocks, o_parts)).astype(BF16)
    d_mixed_theirs = sum(mm(b, w) for b, w in zip(d_blocks, o_others)).astype(BF16)
    d_mixed = by_core(d_mixed_mine, d_mixed_theirs, 1)

    d_q, d_kv = local_call(
        functools.partial(attend_back_kernel, scale=scale, **shape),
        [((local_len, nq), F32), ((nkeys, 2 * nkv), F32)],
        q_rot,
        kv_ext,
        d_mixed,
        seg_q[None],
        seg_k[:, None],
    )
    d_kv_loc = d_kv[nhalo * local_len :]
    for s in range(1, nhalo + 1):
        lo = (nhalo - s) * local_len
        piece = d_kv[lo : lo + local_len].astype(BF16)
        piece = lax.ppermute(piece, HEADS, [(i + s, i) for i in range(nh - s)])
        d_kv_loc = d_kv_loc + piece.astype(F32)

    def unrotate(d, nrot, start):
        return local_call(
            functools.partial(unrotate_kernel, nrot=nrot, start=start),
            [(d.shape, BF16), ((1, PAIR), F32)],
            d,
            qkv,
            cos,
            sin,
            gains,
        )

    d_q_raw, g_qgain = unrotate(d_q, q_heads, 0)
    d_kv_raw, g_kgain = unrotate(d_kv_loc, kv_heads, nq)
    g_qgain = g_qgain[0, :HD] + g_qgain[0, HD:]
    g_kgain = g_kgain[0, :HD] + g_kgain[0, HD:]
    spare = jnp.zeros((local_len, npad), BF16)
    d_mine, d_theirs = core_cols(jnp.concatenate([d_q_raw, d_kv_raw, spare], axis=1))
    gq_theirs = dot_tn(normed, d_theirs)
    gq_mine = dot_tn(normed, d_mine)
    r_qkv = scatter_grad(gq_mine, gq_theirs)
    d_normed = dot_nt(d_mine, qkv_part)
    d_normed = d_normed + dot_nt(d_theirs, qkv_other)
    g_attn = jnp.sum(d_normed * unit_one, axis=0)
    grad_in = (
        (d_resid + norm_back(d_normed, unit_one, inv_one, attn_gain))
        .astype(BF16)
        .reshape(groups, local_len, width)
    )
    small = all_sum(jnp.concatenate([g_attn, g_ffn, g_qgain, g_kgain]))
    nz = lax.axis_size(ZZ)
    at = ((h * nz + lax.axis_index(ZZ)) * 2 + lax.axis_index(CORE)) * shard
    r_attn = lax.dynamic_slice_in_dim(small, at, shard, 0)
    r_ffn = lax.dynamic_slice_in_dim(small, width + at, shard, 0)
    return (
        layer_out,
        grad_in,
        r_attn,
        r_qkv[:, :nq],
        r_qkv[:, nq : nq + nkv],
        r_qkv[:, nq + nkv : nq + 2 * nkv],
        small[2 * width : 2 * width + HD],
        small[2 * width + HD :],
        r_out,
        r_ffn,
        r_gate,
        r_up,
        r_down,
    )


def solution(mesh):
    nh, nr = mesh.shape[HEADS], mesh.shape["rows"]
    fine = Mesh(mesh.devices.reshape(nh, nr // 2, 2), ALL)
    tokens = P(ROWS, HEADS, None)
    weight = P(ALL, None)
    vector = P(ALL)
    in_specs = (
        tokens,
        P(ROWS, None),
        P(),
        weight,
        weight,
        weight,
        P(),
        P(),
        weight,
        P(),
        weight,
        weight,
        weight,
        tokens,
    )
    out_specs = (
        tokens,
        tokens,
        vector,
        weight,
        weight,
        weight,
        P(),
        P(),
        weight,
        vector,
        weight,
        weight,
        weight,
    )

    return jax.shard_map(
        shards, mesh=fine, in_specs=in_specs, out_specs=out_specs, check_vma=False
    )
```
